32 devices in a mesh: mx: 8 (over y, x, core), my: 4 (over z).
Axes of the slice: x: 2, y: 2, z: 4, core: 2. Of those that a mesh axis runs over, the one named last changes fastest.
Arguments:
- positions: float32 [3, 4096], P(None, ('mx', 'my')), may hold values from -6 to 6
- velocities: float32 [3, 4096], P(None, ('mx', 'my')), may hold values from -6 to 6
- rest_positions: float32 [3, 4096], P(None, ('mx', 'my')), may hold values from -6 to 6
- inverse_mass: float32 [4096], P(('mx', 'my')), may hold values from 0.5 to 2
- element_nodes: int32 [8, 8192], P(None, ('mx', 'my')), may hold values from 0 to 127
- modulus: float32 [8192], P(('mx', 'my')), may hold values from 0.1 to 1
- stiffness: float32 [24, 24], replicated, may hold values from -0.7 to 4.7
- shared_lists: int32 [4, 4096], P(None, ('mx', 'my')), may hold values from 0 to 127
- patch_nodes: int32 [512, 128], P(('mx', 'my')), may hold values from 0 to 127
- patch_owner: int32 [512], P(('mx', 'my')), may hold values from 0 to 3, as said below
- pair_map: int32 [512, 128], P(('mx', 'my')), may hold values from 0 to 127
Outputs:
- new_positions: float32 [3, 4096], P(None, ('mx', 'my'))
- new_velocities: float32 [3, 4096], P(None, ('mx', 'my'))
The draws below stay inside these ranges and needn't reach their ends.
Inputs may be any that keep to these rules, and one draw needn't show every extreme that they name: `patch_owner`: on every device, at most 8 of its 16 patches name one owner, and exactly 8 name some owner.
All inputs are finite; a program needn't handle non-finite values.
Results may differ from the reference program's by a relative error of at most 0.0003.
Values sent between devices are 32-bit elements; how exact they have to be, the bound alone decides.
No kernel may reach another device: no remote copies, remote signals or barrier semaphores. Data moves between devices by JAX's collectives and lax.ppermute only.
A program may use at most 64 MiB of HBM per device.

```python
import math
import jax
import jax.numpy as jnp
from jax import lax

NODE_DEV = 128
ELEM_DEV = 256
PATCH_DEV = 16
FACE = 128
PATCH = 128
STEPS = 2
CAP = 8
NODES = 4096
ELEMS = 8192
PATCHES = 512
FACES = 4096
N_MX = 8
N_MY = 4
DEVICES = 32


def draw_patch_owner(key, part):

    def per_device(device_key):
        key_hot, key_rest, key_order = jax.random.split(device_key, 3)
        hottest = jax.random.randint(key_hot, (), 0, max(1, N_MY // 4), dtype=jnp.int32)
        others = jnp.arange((N_MY - 1) * CAP, dtype=jnp.int32) // CAP
        others = others + (others >= hottest).astype(jnp.int32)
        others = jax.random.permutation(key_rest, others)
        sequence = jnp.concatenate([jnp.full((CAP,), hottest, jnp.int32), others[:PATCH_DEV - CAP]])
        return jax.random.permutation(key_order, sequence)
    device_keys = jax.random.split(jax.random.fold_in(key, 7), DEVICES)
    return jax.vmap(per_device)(device_keys).reshape(DEVICES * PATCH_DEV)


def draw_stiffness(key, part):
    key_rows, key_diag = jax.random.split(jax.random.fold_in(key, 11))
    entries = jax.random.uniform(key_rows, (24, 24), jnp.float32, -1.0, 1.0)
    symmetric = 0.35 * (entries + entries.T)
    return symmetric + jnp.diag(jax.random.uniform(key_diag, (24,), jnp.float32, 2.0, 4.0))


def with_ends(drawn, rng, least, largest):
    longest = drawn.shape.index(max(drawn.shape))
    spots = []
    for shift in (0, 1):
        where = [jax.random.randint(jax.random.fold_in(rng, axis), (), 0, length) for axis, length in enumerate(drawn.shape)]
        where[longest] = (where[longest] + shift) % drawn.shape[longest]
        spots.append(tuple(where))
    return drawn.at[spots[0]].set(least).at[spots[1]].set(largest)


def block_scale(stream_key, shape, cuts, low, high):
    def one(position, shards_of):
        heights = jax.random.uniform(jax.random.fold_in(jax.random.fold_in(stream_key, 6), position), (shards_of,), jnp.float32, low / len(cuts), high / len(cuts))
        return jnp.repeat(jnp.exp(heights), shape[position] // shards_of).reshape((-1,) + (1,) * (len(shape) - position - 1))

    gain = one(*cuts[0])
    for cut in cuts[1:]:
        gain = gain * one(*cut)
    return gain


def gaussian(own_key, shape, scale, bound, cuts=(), kind=jnp.bfloat16):
    gain = block_scale(own_key, shape, cuts, -0.22, 0.18) if cuts else 1.0
    drawn = jax.random.normal(own_key, shape, jnp.float32) * scale * gain
    return jnp.minimum(jnp.maximum(drawn, -bound), bound).astype(kind)


def setup_inputs(seed: int = 0) -> dict:
    key_of = jax.random.split(jax.random.key(seed), 12)
    return {
        "positions": gaussian(key_of[0], (3, NODES), 1.0, 6.0, ((1, 32),), jnp.float32),
        "velocities": gaussian(key_of[1], (3, NODES), 1.0, 6.0, ((1, 32),), jnp.float32),
        "rest_positions": gaussian(key_of[2], (3, NODES), 1.0, 6.0, ((1, 32),), jnp.float32),
        "inverse_mass": jnp.clip(jnp.exp(math.log(2.0) - 1.3862944 * jax.random.uniform(key_of[3], (NODES,), jnp.float32) ** block_scale(key_of[3], (NODES,), ((0, 32),), -0.2, 0.2)), 0.5, 2.0),
        "element_nodes": with_ends(jax.random.randint(key_of[4], (8, ELEMS), 0, NODE_DEV), jax.random.fold_in(key_of[4], 1), 0, NODE_DEV - 1).astype(jnp.int32),
        "modulus": jnp.clip(jnp.exp(math.log(1.0) - 2.3025851 * jax.random.uniform(key_of[5], (ELEMS,), jnp.float32) ** block_scale(key_of[5], (ELEMS,), ((0, 32),), -0.2, 0.2)), 0.1, 1.0),
        "stiffness": draw_stiffness(jax.random.fold_in(key_of[11], 71), 0),
        "shared_lists": with_ends(jax.random.randint(key_of[7], (4, FACES), 0, NODE_DEV), jax.random.fold_in(key_of[7], 1), 0, NODE_DEV - 1).astype(jnp.int32),
        "patch_nodes": with_ends(jax.random.randint(key_of[8], (PATCHES, PATCH), 0, NODE_DEV), jax.random.fold_in(key_of[8], 1), 0, NODE_DEV - 1).astype(jnp.int32),
        "patch_owner": draw_patch_owner(jax.random.fold_in(key_of[11], 71), 0),
        "pair_map": with_ends(jax.random.randint(key_of[10], (PATCHES, PATCH), 0, PATCH), jax.random.fold_in(key_of[10], 1), 0, PATCH - 1).astype(jnp.int32),
    }


time_step = 0.1
penalty = 4.0
damping = 0.5
contact_reach = 4.0


def element_forces(displaced, element_nodes, modulus, stiffness):
    nodes_count = displaced.shape[1]
    elements_count = element_nodes.shape[1]
    local_disp = displaced[:, element_nodes].reshape(24, elements_count)
    product = jnp.dot(stiffness, local_disp, precision=lax.Precision.HIGHEST)
    forces = -modulus[None, :] * product
    return jnp.zeros((3, nodes_count), jnp.float32).at[:, element_nodes].add(forces.reshape(3, 8, elements_count))


def pair_forces(states, partner):
    offset = partner[:, 0:3] - states[:, 0:3]
    distance = jnp.sum(offset * offset, axis=1, keepdims=True)
    weight = jnp.exp(-distance / contact_reach)
    return -penalty * weight * offset + damping * weight * (partner[:, 3:6] - states[:, 3:6])


def reaction(forces, pairs):
    return jnp.zeros((3, forces.shape[1]), jnp.float32).at[:, pairs].add(-forces)


def row_contact(location, motion, patch_row, owner_row, pair_row):
    def collect(place_block, speed_block, members):
        return jnp.concatenate([place_block[:, members], speed_block[:, members]], axis=0)

    gathered = jax.vmap(collect)(location, motion, patch_row)
    states = gathered.transpose(0, 2, 1, 3).reshape(N_MY * PATCH_DEV, 6, PATCH)
    total_count = states.shape[0]
    order = jnp.arange(total_count, dtype=jnp.int32)
    same = owner_row[:, None] == owner_row[None, :]
    ranked = jnp.where(same, jnp.where(order[None, :] > order[:, None], order[None, :], order[None, :] + total_count), 3 * total_count)
    follower = (jnp.min(ranked, axis=1) % total_count).astype(jnp.int32)
    partner_rows = states[follower]
    indices = jnp.broadcast_to(pair_row[:, None, :], partner_rows.shape)
    partner = jnp.take_along_axis(partner_rows, indices, axis=2)
    forces = pair_forces(states, partner)
    pushes = jax.vmap(reaction)(forces, pair_row)
    total = forces + jnp.zeros_like(forces).at[follower].add(pushes)
    per_device = total.reshape(N_MY, PATCH_DEV, 3, PATCH).transpose(0, 2, 1, 3)

    def spread(piece, members):
        return jnp.zeros((3, NODE_DEV), jnp.float32).at[:, members].add(piece)

    return jax.vmap(spread)(per_device, patch_row)


def row_forces(items, stiffness):
    location, motion, resting, connect, moduli, patch_row, owner_row, pair_row = items
    elastic = jax.vmap(element_forces, in_axes=(0, 0, 0, None))(location - resting, connect, moduli, stiffness)
    return elastic + row_contact(location, motion, patch_row, owner_row, pair_row)


def add_faces(block, lists, low_x, high_x, low_y, high_y):
    block = block.at[:, lists[0]].add(low_x).at[:, lists[1]].add(high_x)
    return block.at[:, lists[2]].add(low_y).at[:, lists[3]].add(high_y)


def shared_sum(assembled, lists):
    values = jax.vmap(jax.vmap(lambda block, faces: block[:, faces]))(assembled, lists)
    blank_x = jnp.zeros_like(values[:1])
    low_x = jnp.concatenate([blank_x, values[:-1]], axis=0)[:, :, :, 1]
    high_x = jnp.concatenate([values[1:], blank_x], axis=0)[:, :, :, 0]
    blank_y = jnp.zeros_like(values[:, :1])
    low_y = jnp.concatenate([blank_y, values[:, :-1]], axis=1)[:, :, :, 3]
    high_y = jnp.concatenate([values[:, 1:], blank_y], axis=1)[:, :, :, 2]
    return jax.vmap(jax.vmap(add_faces))(assembled, lists, low_x, high_x, low_y, high_y)


def split_nodes(array):
    return array.reshape(3, N_MX, N_MY, NODE_DEV).transpose(1, 2, 0, 3)


def reference(positions, velocities, rest_positions, inverse_mass, element_nodes, modulus, stiffness, shared_lists, patch_nodes, patch_owner, pair_map):
    location = split_nodes(positions)
    motion = split_nodes(velocities)
    resting = split_nodes(rest_positions)
    masses = inverse_mass.reshape(N_MX, N_MY, 1, NODE_DEV)
    connect = element_nodes.reshape(8, N_MX, N_MY, ELEM_DEV).transpose(1, 2, 0, 3)
    moduli = modulus.reshape(N_MX, N_MY, ELEM_DEV)
    lists = shared_lists.reshape(4, N_MX, N_MY, FACE).transpose(1, 2, 0, 3)
    patches = patch_nodes.reshape(N_MX, N_MY, PATCH_DEV, PATCH)
    owners = patch_owner.reshape(N_MX, N_MY * PATCH_DEV)
    pairs = pair_map.reshape(N_MX, N_MY * PATCH_DEV, PATCH)
    for section in range(STEPS):
        assembled = lax.map(lambda items: row_forces(items, stiffness), (location, motion, resting, connect, moduli, patches, owners, pairs))
        total = shared_sum(assembled, lists)
        motion = motion + time_step * masses * total
        location = location + time_step * motion
    merged_positions = location.transpose(2, 0, 1, 3).reshape(3, N_MX * N_MY * NODE_DEV)
    merged_velocities = motion.transpose(2, 0, 1, 3).reshape(3, N_MX * N_MY * NODE_DEV)
    return merged_positions, merged_velocities
```

```python
import functools

import jax
import jax.numpy as jnp
from jax import lax
from jax.experimental import pallas as pl
from jax.experimental.pallas import tpu as pltpu
from jax.sharding import PartitionSpec as P

STEPS = 2

time_step = 0.1
penalty = 4.0
damping = 0.5
contact_reach = 4.0
exact = lax.Precision.HIGHEST
LANES = 128
TILE = 8
ROW_MASS, ROW_SPEED, ROW_OWNER, ROW_ELASTIC, ROW_LISTS, ROW_PATCH = 3, 4, 7, 8, 12, 16


def pick(rows, indices):
    return jnp.take_along_axis(rows, indices, axis=1)


def spots(row):
    nodes = lax.broadcasted_iota(jnp.int32, (LANES, row.shape[1]), 0)
    return jnp.where(nodes == row, 1.0, 0.0).astype(jnp.bfloat16)


def put_parts(parts_ref, values, rows, base=0):
    for c, value in enumerate(values):
        high = value.astype(jnp.bfloat16).astype(jnp.float32)
        parts_ref[base + c * rows : base + (c + 1) * rows, :] = high
        parts_ref[base + (4 + c) * rows : base + (5 + c) * rows, :] = value - high


def fold(product):
    turned = product.T
    return turned + pltpu.roll(turned, 4, 0)


def scatter(hot, weights):
    return fold(
        lax.dot_general(hot, weights, (((1,), (1,)), ((), ())), preferred_element_type=jnp.float32)
    )


def tile_parts(tile):
    high = tile.astype(jnp.bfloat16).astype(jnp.float32)
    rest = pltpu.roll(tile - high, 4, 0)
    row = lax.broadcasted_iota(jnp.int32, tile.shape, 0)
    return jnp.where(row < 4, high, rest).astype(jnp.bfloat16)


def elastic_terms(place, rest, connect, modulus, stiffness, parts_ref, hot_ref, weight_ref):
    corners, count = connect.shape
    moved = place - rest
    local = jnp.concatenate(
        [
            jnp.concatenate(
                [
                    pick(
                        jnp.broadcast_to(moved[c : c + 1], (corners, LANES)),
                        connect[:, k * LANES : (k + 1) * LANES],
                    )
                    for k in range(count // LANES)
                ],
                axis=1,
            )
            for c in range(3)
        ],
        axis=0,
    )
    product = jnp.dot(stiffness, local, precision=exact, preferred_element_type=jnp.float32)
    forces = -modulus * product
    for k in range(count // LANES):
        put_parts(
            parts_ref,
            [forces[c * corners : (c + 1) * corners, k * LANES : (k + 1) * LANES] for c in range(3)],
            corners,
            k * TILE * corners,
        )
    for a in range(corners):
        span = pl.ds(a * count, count)
        hot_ref[:, span] = spots(connect[a : a + 1])
        for k in range(count // LANES):
            weight_ref[:, pl.ds(a * count + k * LANES, LANES)] = parts_ref[
                pl.ds(k * TILE * corners + a, TILE, stride=corners), :
            ].astype(jnp.bfloat16)


def pair_forces(mine, partner):
    offset = [b - a for a, b in zip(mine[:3], partner[:3])]
    distance = offset[0] * offset[0] + offset[1] * offset[1] + offset[2] * offset[2]
    weight = jnp.exp(-distance / contact_reach)
    return [
        -penalty * weight * o + damping * weight * (b - a)
        for o, a, b in zip(offset, mine[3:], partner[3:])
    ]


def choose(rows, device):
    chosen = jnp.broadcast_to(rows[0], device.shape)
    for d, row in enumerate(rows[1:], 1):
        chosen = jnp.where(device == d, row, chosen)
    return chosen


def pack_kernel(
    place_ref, speed_ref, rest_ref, mass_ref, connect_ref, modulus_ref, stiff_ref, lists_ref, patch_ref, owner_ref,
    map_ref, out_ref, parts_ref, hot_ref, weight_ref,
):
    patches = patch_ref.shape[0]
    elastic_terms(
        place_ref[...], rest_ref[...], connect_ref[...], modulus_ref[...], stiff_ref[...], parts_ref, hot_ref, weight_ref
    )
    out_ref[ROW_ELASTIC : ROW_ELASTIC + TILE, :] = scatter(hot_ref[...], weight_ref[...])
    out_ref[0:3, :] = place_ref[...]
    out_ref[ROW_MASS : ROW_MASS + 1, :] = mass_ref[...]
    out_ref[ROW_SPEED : ROW_SPEED + 3, :] = speed_ref[...]
    out_ref[ROW_OWNER : ROW_OWNER + 1, :] = jnp.zeros((1, LANES), jnp.float32)
    out_ref[ROW_OWNER : ROW_OWNER + 1, 0:patches] = owner_ref[...].astype(jnp.float32)
    out_ref[ROW_LISTS : ROW_LISTS + 4, :] = lists_ref[...].astype(jnp.float32)
    out_ref[ROW_PATCH : ROW_PATCH + patches, :] = patch_ref[...].astype(jnp.float32)
    out_ref[ROW_PATCH + patches :, :] = map_ref[...].astype(jnp.float32)


def row_kernel(width, patches, row_ref, total_ref, pair_ref, other_ref, table_ref, parts_ref, back_ref, idx_ref, hot_ref, weight_ref):
    me = lax.axis_index("my")
    side = lax.rem(lax.axis_index("mx"), 2)
    count = width * patches
    slot = [jnp.bitwise_xor(me, u) for u in range(width)]
    state = [row_ref[slot[u], 0:TILE, :] for u in range(width)]
    nodes = jnp.concatenate([row_ref[slot[u], ROW_PATCH : ROW_PATCH + patches, :] for u in range(width)], axis=0)
    pairs = jnp.concatenate([row_ref[slot[u], ROW_PATCH + patches :, :] for u in range(width)], axis=0)
    lane = lax.broadcasted_iota(jnp.int32, (patches, LANES), 1)
    line = lax.broadcasted_iota(jnp.int32, (patches, LANES), 0)
    owner_col = jnp.concatenate(
        [
            jnp.sum(jnp.where(lane == line, state[u][ROW_OWNER : ROW_OWNER + 1], 0.0), axis=1, keepdims=True)
            for u in range(width)
        ],
        axis=0,
    )
    p = lax.broadcasted_iota(jnp.int32, (count, count), 0).astype(jnp.float32)
    q = lax.broadcasted_iota(jnp.int32, (count, count), 1).astype(jnp.float32)
    owner_row = jnp.sum(jnp.where(p == q, owner_col, 0.0), axis=0, keepdims=True)
    same = owner_col == owner_row
    after = jnp.min(jnp.where(same, jnp.where(q > p, q, q + count), 3.0 * count), axis=1, keepdims=True)
    after = jnp.where(after >= count, after - count, after)
    before = jnp.max(jnp.where(same, jnp.where(q < p, q + count, q), -1.0), axis=1, keepdims=True)
    before = jnp.where(before >= count, before - count, before)
    link = jnp.where(q == after, 1.0, 0.0).astype(jnp.bfloat16)
    back = jnp.where(q == before, 1.0, 0.0).astype(jnp.bfloat16)

    def route(table, rows):
        return jnp.dot(table, rows.astype(jnp.bfloat16), preferred_element_type=jnp.float32)

    target = pick(route(link, nodes), pairs.astype(jnp.int32))
    device = jnp.broadcast_to(jnp.floor(after / patches), (count, LANES))
    node_ids, target_ids = nodes.astype(jnp.int32), target.astype(jnp.int32)
    device_ids = device.astype(jnp.int32)
    mine, partner = [], []
    for c in (0, 1, 2, 4, 5, 6):
        rows = [state[u][c : c + 1] for u in range(width)]
        own = jnp.concatenate([jnp.broadcast_to(row, (patches, LANES)) for row in rows], axis=0)
        mine.append(pick(own, node_ids))
        partner.append(pick(choose(rows, device_ids), target_ids))
    forces = pair_forces(mine, partner)
    put_parts(parts_ref, forces, count)
    for g in (0, 1, 2, 4, 5, 6):
        back_ref[g * count : (g + 1) * count, :] = -route(back, parts_ref[g * count : (g + 1) * count, :])
    landing = route(back, target)
    from_nodes = route(back, nodes)
    idx_ref[0:count, :] = node_ids
    idx_ref[count : 2 * count, :] = landing.astype(jnp.int32)
    idx_ref[2 * count : 3 * count, :] = target_ids
    idx_ref[3 * count : 4 * count, :] = from_nodes.astype(jnp.int32)
    idx_ref[4 * count : 5 * count, :] = device_ids
    idx_ref[5 * count : 6 * count, :] = jnp.broadcast_to(jnp.floor(before / patches), (count, LANES)).astype(jnp.int32)
    for g in range(6):
        table_ref[g * patches : (g + 1) * patches, :] = idx_ref[pl.ds(g * count + me * patches, patches), :]

    def unit(u):
        for s in range(patches):
            at = u * patches + s
            hot_ref[:, s * LANES : (s + 1) * LANES] = spots(idx_ref[pl.ds(at, 1), :])
            weight_ref[:, s * LANES : (s + 1) * LANES] = parts_ref[pl.ds(at, TILE, stride=count), :].astype(jnp.bfloat16)
            far = patches + s
            hot_ref[:, far * LANES : (far + 1) * LANES] = spots(idx_ref[pl.ds(count + at, 1), :])
            weight_ref[:, far * LANES : (far + 1) * LANES] = back_ref[pl.ds(at, TILE, stride=count), :].astype(jnp.bfloat16)
        place = jnp.bitwise_xor(me, u)
        info = row_ref[place, ROW_ELASTIC : ROW_ELASTIC + TILE, :]
        total = scatter(hot_ref[...], weight_ref[...]) + info
        total_ref[u] = total
        lists = info.astype(jnp.int32)
        low = pick(total, jnp.broadcast_to(lists[4:5], (TILE, LANES)))
        high = pick(total, jnp.broadcast_to(lists[5:6], (TILE, LANES)))
        pair_ref[u] = jnp.where(side == 0, high, low)[0:4]
        other_ref[u] = jnp.where(side == 0, low, high)[0:4]

    if width <= 4:
        for u in range(width):
            unit(u)
    else:
        lax.fori_loop(0, width, lambda u, carry: (unit(u), carry)[1], 0)


def faces(tiles, lists, hot_ref, weight_ref):
    for k, tile in enumerate(tiles):
        hot_ref[:, k * LANES : (k + 1) * LANES] = spots(lists[k])
        weight_ref[:, k * LANES : (k + 1) * LANES] = tile_parts(tile)
    return scatter(hot_ref[:, 0 : len(tiles) * LANES], weight_ref[:, 0 : len(tiles) * LANES])


def step_kernel(
    width, patches, row_ref, total_ref, pair_ref, other_ref, table_ref, rest_ref, connect_ref, modulus_ref, stiff_ref,
    state_ref, near_ref, send_ref, next_ref, fparts_ref, parts_ref, hot_ref, weight_ref,
):
    me = lax.axis_index("my")
    side = lax.rem(lax.axis_index("mx"), 2)
    blank = jnp.zeros((4, LANES), jnp.float32)

    def unit(u):
        info = row_ref[jnp.bitwise_xor(me, u), 0 : 2 * TILE, :]
        lists = info[TILE:].astype(jnp.int32)
        lower, upper = lists[4:5], lists[5:6]
        down, up = jnp.maximum(u - 1, 0), jnp.minimum(u + 1, width - 1)
        down_list = row_ref[jnp.bitwise_xor(me, down), ROW_LISTS + 3 : ROW_LISTS + 4, :].astype(jnp.int32)
        up_list = row_ref[jnp.bitwise_xor(me, up), ROW_LISTS + 2 : ROW_LISTS + 3, :].astype(jnp.int32)
        low = pick(total_ref[down], jnp.broadcast_to(down_list, (TILE, LANES)))
        high = pick(total_ref[up], jnp.broadcast_to(up_list, (TILE, LANES)))
        low = jnp.where(u > 0, low, 0.0)
        high = jnp.where(u < width - 1, high, 0.0)
        tiles = [
            jnp.concatenate([pair_ref[u], blank], axis=0),
            jnp.concatenate([other_ref[u], blank], axis=0),
            low,
            high,
        ]
        near, far = jnp.where(side == 0, upper, lower), jnp.where(side == 0, lower, upper)
        total = total_ref[u] + faces(tiles, [near, far, lists[6:7], lists[7:8]], hot_ref, weight_ref)
        speed = info[ROW_SPEED : ROW_SPEED + 3] + time_step * info[ROW_MASS : ROW_MASS + 1] * total[0:3]
        next_ref[u, 0:3, :] = info[0:3] + time_step * speed
        next_ref[u, 4:7, :] = speed

    if width <= 4:
        for u in range(width):
            unit(u)
    else:
        lax.fori_loop(0, width, lambda u, carry: (unit(u), carry)[1], 0)

    own = next_ref[me]
    state_ref[...] = own
    table = [table_ref[g * patches : (g + 1) * patches, :] for g in range(6)]
    nodes, landing, target, from_nodes, to_device, from_device = table
    first, second = [], []
    for c in (0, 1, 2, 4, 5, 6):
        rows = [next_ref[u, c : c + 1, :] for u in range(width)]
        home = jnp.broadcast_to(own[c : c + 1], (patches, LANES))
        first.append(jnp.concatenate([pick(home, nodes), pick(choose(rows, from_device), from_nodes)], axis=0))
        second.append(jnp.concatenate([pick(choose(rows, to_device), target), pick(home, landing)], axis=0))
    forces = pair_forces(first, second)
    sign = jnp.where(lax.broadcasted_iota(jnp.int32, (2 * patches, LANES), 0) < patches, 1.0, -1.0)
    put_parts(parts_ref, [sign * f for f in forces], 2 * patches)
    elastic_terms(
        own[0:3], rest_ref[...], connect_ref[...], modulus_ref[...], stiff_ref[...], fparts_ref, hot_ref, weight_ref
    )
    base = connect_ref.shape[0] * connect_ref.shape[1]
    for s in range(2 * patches):
        span = pl.ds(base + s * LANES, LANES)
        hot_ref[:, span] = spots(table_ref[s : s + 1, :])
        weight_ref[:, span] = parts_ref[pl.ds(s, TILE, stride=2 * patches), :].astype(jnp.bfloat16)
    total = scatter(hot_ref[...], weight_ref[...])
    near_ref[...] = total
    lists = row_ref[0, ROW_ELASTIC : ROW_ELASTIC + TILE, :].astype(jnp.int32)
    sides = [pick(total, jnp.broadcast_to(lists[4 + k : 5 + k], (TILE, LANES))) for k in range(4)]
    even = lax.rem(me, 2) == 0
    send_ref[0] = jnp.where(side == 0, sides[1], sides[0])
    send_ref[1] = jnp.where(side == 0, sides[0], sides[1])
    send_ref[2] = jnp.where(even, sides[3], sides[2])
    send_ref[3] = jnp.where(even, sides[2], sides[3])


def end_kernel(row_ref, state_ref, near_ref, *refs):
    in_refs, (place_ref, speed_ref, hot_ref, weight_ref) = refs[:4], refs[4:]
    side = lax.rem(lax.axis_index("mx"), 2)
    even = lax.rem(lax.axis_index("my"), 2)
    lists = row_ref[0, ROW_ELASTIC : ROW_ELASTIC + TILE, :].astype(jnp.int32)
    order = [
        jnp.where(side == 0, lists[5:6], lists[4:5]),
        jnp.where(side == 0, lists[4:5], lists[5:6]),
        jnp.where(even == 0, lists[7:8], lists[6:7]),
        jnp.where(even == 0, lists[6:7], lists[7:8]),
    ]
    total = near_ref[...] + faces([ref[...] for ref in in_refs], order, hot_ref, weight_ref)
    mass = row_ref[0, ROW_MASS : ROW_MASS + 1, :]
    speed = state_ref[4:7, :] + time_step * mass * total[0:3]
    speed_ref[...] = speed
    place_ref[...] = state_ref[0:3, :] + time_step * speed


def call(kernel, name, outs, scratch, *args):
    return pl.pallas_call(
        kernel,
        name=name,
        out_shape=[jax.ShapeDtypeStruct(shape, jnp.dtype(kind)) for shape, kind in outs],
        in_specs=[pl.BlockSpec(memory_space=pltpu.VMEM)] * len(args),
        out_specs=[pl.BlockSpec(memory_space=pltpu.VMEM)] * len(outs),
        scratch_shapes=[pltpu.VMEM(shape, kind) for shape, kind in scratch],
    )(*args)


def swap(value, axis, first):
    size = lax.axis_size(axis)
    pairs = [(i, i + 1) for i in range(first, size - 1, 2)]
    return lax.ppermute(value, axis, pairs + [(j, i) for i, j in pairs])


def gather_row(record, axis):
    size = lax.axis_size(axis)
    held = record[None]
    step = size // 2
    while step:
        other = lax.ppermute(held, axis, [(i, i ^ step) for i in range(size)])
        held = jnp.stack([held, other], axis=1).reshape((-1,) + record.shape)
        step //= 2
    return held


def body(
    positions, velocities, rest_positions, inverse_mass, element_nodes, modulus, stiffness, shared_lists, patch_nodes,
    patch_owner, pair_map,
):
    width = lax.axis_size("my")
    patches = patch_owner.shape[0]
    corners, elements = element_nodes.shape
    count = width * patches
    spread = corners * elements
    f32, i32, bf16 = jnp.float32, jnp.int32, jnp.bfloat16
    modulus, mass = modulus[None], inverse_mass[None]
    (record,) = call(
        pack_kernel,
        "pack",
        [((ROW_PATCH + 2 * patches, LANES), f32)],
        [((TILE * corners * elements // LANES, LANES), f32), ((LANES, spread), bf16), ((TILE, spread), bf16)],
        positions, velocities, rest_positions, mass, element_nodes, modulus, stiffness, shared_lists, patch_nodes,
        patch_owner[None], pair_map,
    )
    row = gather_row(record, "my")
    total, pair, other, table = call(
        functools.partial(row_kernel, width, patches),
        "row",
        [((width, TILE, LANES), f32), ((width, 4, LANES), f32), ((width, 4, LANES), f32), ((6 * patches, LANES), i32)],
        [
            ((TILE * count, LANES), f32),
            ((TILE * count, LANES), f32),
            ((6 * count, LANES), i32),
            ((LANES, 2 * patches * LANES), bf16),
            ((TILE, 2 * patches * LANES), bf16),
        ],
        row,
    )
    pair, other = swap(pair, "mx", 0), swap(other, "mx", 1)
    deep = spread + 2 * patches * LANES
    state, near, send = call(
        functools.partial(step_kernel, width, patches),
        "step",
        [((TILE, LANES), f32), ((TILE, LANES), f32), ((4, TILE, LANES), f32)],
        [
            ((width, TILE, LANES), f32),
            ((TILE * corners * elements // LANES, LANES), f32),
            ((TILE * 2 * patches, LANES), f32),
            ((LANES, deep), bf16),
            ((TILE, deep), bf16),
        ],
        row, total, pair, other, table, rest_positions, element_nodes, modulus, stiffness,
    )
    arrived = [swap(send[k], axis, first) for k, (axis, first) in enumerate((("mx", 0), ("mx", 1), ("my", 0), ("my", 1)))]
    return tuple(
        call(
            end_kernel,
            "end",
            [((3, LANES), f32), ((3, LANES), f32)],
            [((LANES, 4 * LANES), bf16), ((TILE, 4 * LANES), bf16)],
            row, state, near, *arrived,
        )
    )


def solution(mesh):
    in_specs = (
        P(None, ("mx", "my")),
        P(None, ("mx", "my")),
        P(None, ("mx", "my")),
        P(("mx", "my")),
        P(None, ("mx", "my")),
        P(("mx", "my")),
        P(),
        P(None, ("mx", "my")),
        P(("mx", "my"), None),
        P(("mx", "my")),
        P(("mx", "my"), None),
    )
    out_specs = (P(None, ("mx", "my")), P(None, ("mx", "my")))
    return jax.shard_map(body, mesh=mesh, in_specs=in_specs, out_specs=out_specs, check_vma=False)
```

```python
import functools

import jax
import jax.numpy as jnp
from jax import lax
from jax.experimental import pallas as pl
from jax.experimental.pallas import tpu as pltpu
from jax.sharding import PartitionSpec as P

STEPS = 2

time_step = 0.1
penalty = 4.0
damping = 0.5
contact_reach = 4.0
LANES = 128
TILE = 8
FINE = 32
ROW_MASS, ROW_SPEED, ROW_OWNER, ROW_ELASTIC, ROW_LISTS, ROW_PATCH = 3, 4, 7, 8, 12, 16


def pick(rows, indices):
    return jnp.take_along_axis(rows, indices, axis=1)


def parted(indices):
    coarse = jnp.floor(indices * (1.0 / FINE))
    return coarse, indices - FINE * coarse


def put_parts(parts_ref, values, base=0):
    for c, value in enumerate(values):
        high = value.astype(jnp.bfloat16).astype(jnp.float32)
        rest = value - high
        for b in range(value.shape[0] // TILE):
            at = base + b * TILE * TILE
            parts_ref[at + c * TILE : at + (c + 1) * TILE, :] = high[b * TILE : (b + 1) * TILE]
            parts_ref[at + (4 + c) * TILE : at + (5 + c) * TILE, :] = rest[b * TILE : (b + 1) * TILE]


def get_parts(parts_ref, row):
    if isinstance(row, int):
        start = row // TILE * TILE * TILE + row % TILE
    else:
        start = lax.div(row, TILE) * (TILE * TILE) + lax.rem(row, TILE)
    return parts_ref[pl.ds(start, TILE, stride=TILE), :]


def scatter(entries):
    blocks = LANES // FINE
    total = jnp.zeros((blocks * TILE, FINE), jnp.float32)
    for coarse, fine, weights in entries:
        wide = weights.shape[1]
        shape = (blocks * TILE, wide)
        block = (lax.broadcasted_iota(jnp.int32, shape, 0) // TILE).astype(jnp.float32).astype(jnp.bfloat16)
        placed = jnp.where(
            jnp.broadcast_to(coarse, shape).astype(jnp.bfloat16) == block,
            jnp.concatenate([weights] * blocks, axis=0).astype(jnp.bfloat16),
            jnp.zeros(shape, jnp.bfloat16),
        )
        shape = (FINE, wide)
        node = lax.broadcasted_iota(jnp.int32, shape, 0).astype(jnp.float32).astype(jnp.bfloat16)
        hot = jnp.where(
            jnp.broadcast_to(fine, shape).astype(jnp.bfloat16) == node,
            jnp.ones(shape, jnp.bfloat16),
            jnp.zeros(shape, jnp.bfloat16),
        )
        total += lax.dot_general(placed, hot, (((1,), (1,)), ((), ())), preferred_element_type=jnp.float32)
    tile = jnp.concatenate([total[b * TILE : (b + 1) * TILE] for b in range(blocks)], axis=1)
    return tile + pltpu.roll(tile, 4, 0)


def joined(entries):
    return [
        tuple(jnp.concatenate([a, b], axis=1) for a, b in zip(*two)) for two in zip(entries[0::2], entries[1::2])
    ]


def tile_parts(tile):
    high = tile.astype(jnp.bfloat16).astype(jnp.float32)
    rest = pltpu.roll(tile - high, 4, 0)
    row = lax.broadcasted_iota(jnp.int32, tile.shape, 0)
    return jnp.where(row < 4, high, rest)


def product(left, right):
    def parts(x):
        high = x.astype(jnp.bfloat16)
        return high, (x - high.astype(jnp.float32)).astype(jnp.bfloat16)

    (lh, lr), (rh, rr) = parts(left), parts(right)
    return sum(jnp.dot(a, b, preferred_element_type=jnp.float32) for a, b in ((lh, rh), (lr, rh), (lh, rr)))


def elastic_terms(place, rest, connect, modulus, stiffness, parts_ref):
    corners, count = connect.shape
    moved = place - rest
    local = jnp.concatenate(
        [
            jnp.concatenate(
                [
                    pick(
                        jnp.broadcast_to(moved[c : c + 1], (corners, LANES)),
                        connect[:, k * LANES : (k + 1) * LANES],
                    )
                    for k in range(count // LANES)
                ],
                axis=1,
            )
            for c in range(3)
        ],
        axis=0,
    )
    forces = -modulus * product(stiffness, local)
    for k in range(count // LANES):
        put_parts(
            parts_ref,
            [forces[c * corners : (c + 1) * corners, k * LANES : (k + 1) * LANES] for c in range(3)],
            k * corners * TILE,
        )
    coarse, fine = parted(connect.astype(jnp.float32))
    return [
        (
            coarse[a : a + 1],
            fine[a : a + 1],
            jnp.concatenate([get_parts(parts_ref, k * corners + a) for k in range(count // LANES)], axis=1),
        )
        for a in range(corners)
    ]


def pair_forces(mine, partner):
    offset = [b - a for a, b in zip(mine[:3], partner[:3])]
    distance = offset[0] * offset[0] + offset[1] * offset[1] + offset[2] * offset[2]
    weight = jnp.exp(-distance / contact_reach)
    return [
        -penalty * weight * o + damping * weight * (b - a)
        for o, a, b in zip(offset, mine[3:], partner[3:])
    ]


def choose(rows, device):
    chosen = jnp.broadcast_to(rows[0], device.shape)
    for d, row in enumerate(rows[1:], 1):
        chosen = jnp.where(device == d, row, chosen)
    return chosen


def pack_kernel(
    place_ref, speed_ref, rest_ref, mass_ref, connect_ref, modulus_ref, stiff_ref, lists_ref, patch_ref, owner_ref,
    map_ref, out_ref, *refs,
):
    patches = patch_ref.shape[0]
    keep_refs, (parts_ref,) = refs[:-1], refs[-1:]
    for keep_ref, ref in zip(keep_refs, (rest_ref, connect_ref, modulus_ref, stiff_ref)):
        keep_ref[...] = ref[...].astype(jnp.float32)
    out_ref[ROW_ELASTIC : ROW_ELASTIC + TILE, :] = scatter(
        elastic_terms(place_ref[...], rest_ref[...], connect_ref[...], modulus_ref[...], stiff_ref[...], parts_ref)
    )
    out_ref[0:3, :] = place_ref[...]
    out_ref[ROW_MASS : ROW_MASS + 1, :] = mass_ref[...]
    out_ref[ROW_SPEED : ROW_SPEED + 3, :] = speed_ref[...]
    out_ref[ROW_OWNER : ROW_OWNER + 1, :] = jnp.zeros((1, LANES), jnp.float32)
    out_ref[ROW_OWNER : ROW_OWNER + 1, 0:patches] = owner_ref[...].astype(jnp.float32)
    out_ref[ROW_LISTS : ROW_LISTS + 4, :] = lists_ref[...].astype(jnp.float32)
    out_ref[ROW_PATCH : ROW_PATCH + patches, :] = patch_ref[...].astype(jnp.float32)
    out_ref[ROW_PATCH + patches :, :] = map_ref[...].astype(jnp.float32)


def row_kernel(width, patches, row_ref, total_ref, pair_ref, other_ref, table_ref, parts_ref, back_ref, idx_ref, coarse_ref, fine_ref):
    me = lax.axis_index("my")
    side = lax.rem(lax.axis_index("mx"), 2)
    count = width * patches
    slot = [slot_of(me, u, width) for u in range(width)]
    state = [row_ref[slot[u], 0:TILE, :] for u in range(width)]
    nodes = jnp.concatenate([row_ref[slot[u], ROW_PATCH : ROW_PATCH + patches, :] for u in range(width)], axis=0)
    pairs = jnp.concatenate([row_ref[slot[u], ROW_PATCH + patches :, :] for u in range(width)], axis=0)
    lane = lax.broadcasted_iota(jnp.int32, (patches, LANES), 1)
    line = lax.broadcasted_iota(jnp.int32, (patches, LANES), 0)
    owner_col = jnp.concatenate(
        [
            jnp.sum(jnp.where(lane == line, state[u][ROW_OWNER : ROW_OWNER + 1], 0.0), axis=1, keepdims=True)
            for u in range(width)
        ],
        axis=0,
    )
    p = lax.broadcasted_iota(jnp.int32, (count, count), 0).astype(jnp.float32)
    q = lax.broadcasted_iota(jnp.int32, (count, count), 1).astype(jnp.float32)
    owner_row = jnp.sum(jnp.where(p == q, owner_col, 0.0), axis=0, keepdims=True)
    same = owner_col == owner_row
    after = jnp.min(jnp.where(same, jnp.where(q > p, q, q + count), 3.0 * count), axis=1, keepdims=True)
    after = jnp.where(after >= count, after - count, after)
    before = jnp.max(jnp.where(same, jnp.where(q < p, q + count, q), -1.0), axis=1, keepdims=True)
    before = jnp.where(before >= count, before - count, before)
    link = jnp.where(q == after, 1.0, 0.0).astype(jnp.bfloat16)
    back = jnp.where(q == before, 1.0, 0.0).astype(jnp.bfloat16)

    def route(table, rows):
        return jnp.dot(table, rows.astype(jnp.bfloat16), preferred_element_type=jnp.float32)

    target = pick(route(link, nodes), pairs.astype(jnp.int32))
    device = jnp.broadcast_to(jnp.floor(after / patches), (count, LANES))
    node_ids, target_ids = nodes.astype(jnp.int32), target.astype(jnp.int32)
    device_ids = device.astype(jnp.int32)
    mine, partner = [], []
    for c in (0, 1, 2, 4, 5, 6):
        rows = [state[u][c : c + 1] for u in range(width)]
        own = jnp.concatenate([jnp.broadcast_to(row, (patches, LANES)) for row in rows], axis=0)
        mine.append(pick(own, node_ids))
        partner.append(pick(choose(rows, device_ids), target_ids))
    forces = pair_forces(mine, partner)
    put_parts(parts_ref, forces)
    for c, force in enumerate(forces):
        high = force.astype(jnp.bfloat16).astype(jnp.float32)
        for g, part in ((c, high), (4 + c, force - high)):
            routed = -route(back, part)
            for b in range(count // TILE):
                at = b * TILE * TILE + g * TILE
                back_ref[at : at + TILE, :] = routed[b * TILE : (b + 1) * TILE]
    landing = route(back, target)
    from_nodes = route(back, nodes)
    idx_ref[0:count, :] = nodes
    idx_ref[count : 2 * count, :] = landing
    idx_ref[2 * count : 3 * count, :] = target
    idx_ref[3 * count : 4 * count, :] = from_nodes
    idx_ref[4 * count : 5 * count, :] = device
    idx_ref[5 * count : 6 * count, :] = jnp.broadcast_to(jnp.floor(before / patches), (count, LANES))
    for g in range(6):
        table_ref[g * patches : (g + 1) * patches, :] = idx_ref[pl.ds(g * count + me * patches, patches), :]
    coarse, fine = parted(idx_ref[0 : 2 * count, :])
    coarse_ref[...] = coarse
    fine_ref[...] = fine

    def unit(u):
        entries = []
        for base, ref in ((0, parts_ref), (count, back_ref)):
            for s in range(patches):
                at = u * patches + s
                entries.append(
                    (
                        coarse_ref[pl.ds(base + at, 1), :],
                        fine_ref[pl.ds(base + at, 1), :],
                        get_parts(ref, at),
                    )
                )
        info = row_ref[slot_of(me, u, width), ROW_ELASTIC : ROW_ELASTIC + TILE, :]
        total = scatter(joined(entries)) + info
        total_ref[u] = total
        lists = info.astype(jnp.int32)
        low = pick(total, jnp.broadcast_to(lists[4:5], (TILE, LANES)))
        high = pick(total, jnp.broadcast_to(lists[5:6], (TILE, LANES)))
        pair_ref[u] = jnp.where(side == 0, high, low)[0:4]
        other_ref[u] = jnp.where(side == 0, low, high)[0:4]

    if width <= 4:
        for u in range(width):
            unit(u)
    else:
        lax.fori_loop(0, width, lambda u, carry: (unit(u), carry)[1], 0)


def faces(tiles, lists):
    return scatter(joined([(*parted(row), tile_parts(tile)) for row, tile in zip(lists, tiles)]))


def step_kernel(
    width, patches, row_ref, total_ref, pair_ref, other_ref, table_ref, rest_ref, connect_ref, modulus_ref, stiff_ref,
    state_ref, near_ref, *refs,
):
    send_refs, (next_ref, fparts_ref, parts_ref) = refs[:4], refs[4:]
    me = lax.axis_index("my")
    side = lax.rem(lax.axis_index("mx"), 2)
    blank = jnp.zeros((4, LANES), jnp.float32)

    def unit(u):
        info = row_ref[slot_of(me, u, width), 0 : 2 * TILE, :]
        lists = info[TILE:]
        lower, upper = lists[4:5], lists[5:6]
        down, up = jnp.maximum(u - 1, 0), jnp.minimum(u + 1, width - 1)
        down_list = row_ref[slot_of(me, down, width), ROW_LISTS + 3 : ROW_LISTS + 4, :].astype(jnp.int32)
        up_list = row_ref[slot_of(me, up, width), ROW_LISTS + 2 : ROW_LISTS + 3, :].astype(jnp.int32)
        low = pick(total_ref[down], jnp.broadcast_to(down_list, (TILE, LANES)))
        high = pick(total_ref[up], jnp.broadcast_to(up_list, (TILE, LANES)))
        low = jnp.where(u > 0, low, 0.0)
        high = jnp.where(u < width - 1, high, 0.0)
        tiles = [
            jnp.concatenate([pair_ref[u], blank], axis=0),
            jnp.concatenate([other_ref[u], blank], axis=0),
            low,
            high,
        ]
        near, far = jnp.where(side == 0, upper, lower), jnp.where(side == 0, lower, upper)
        total = total_ref[u] + faces(tiles, [near, far, lists[6:7], lists[7:8]])
        speed = info[ROW_SPEED : ROW_SPEED + 3] + time_step * info[ROW_MASS : ROW_MASS + 1] * total[0:3]
        next_ref[u, 0:3, :] = info[0:3] + time_step * speed
        next_ref[u, 4:7, :] = speed

    if width <= 4:
        for u in range(width):
            unit(u)
    else:
        lax.fori_loop(0, width, lambda u, carry: (unit(u), carry)[1], 0)

    own = next_ref[me]
    state_ref[...] = own
    table = [table_ref[g * patches : (g + 1) * patches, :].astype(jnp.int32) for g in range(6)]
    nodes, landing, target, from_nodes, to_device, from_device = table
    first, second = [], []
    for c in (0, 1, 2, 4, 5, 6):
        rows = [next_ref[u, c : c + 1, :] for u in range(width)]
        home = jnp.broadcast_to(own[c : c + 1], (patches, LANES))
        first.append(jnp.concatenate([pick(home, nodes), pick(choose(rows, from_device), from_nodes)], axis=0))
        second.append(jnp.concatenate([pick(choose(rows, to_device), target), pick(home, landing)], axis=0))
    forces = pair_forces(first, second)
    sign = jnp.where(lax.broadcasted_iota(jnp.int32, (2 * patches, LANES), 0) < patches, 1.0, -1.0)
    put_parts(parts_ref, [sign * f for f in forces])
    coarse, fine = parted(table_ref[0 : 2 * patches, :])
    entries = [
        (coarse[s : s + 1], fine[s : s + 1], get_parts(parts_ref, s))
        for s in range(2 * patches)
    ]
    total = scatter(
        elastic_terms(own[0:3], rest_ref[...], connect_ref[...].astype(jnp.int32), modulus_ref[...], stiff_ref[...], fparts_ref)
        + joined(entries)
    )
    near_ref[...] = total
    lists = row_ref[0, ROW_ELASTIC : ROW_ELASTIC + TILE, :].astype(jnp.int32)
    sides = [pick(total, jnp.broadcast_to(lists[4 + k : 5 + k], (TILE, LANES))) for k in range(4)]
    even = lax.rem(me, 2) == 0
    send_refs[0][...] = jnp.where(side == 0, sides[1], sides[0])
    send_refs[1][...] = jnp.where(side == 0, sides[0], sides[1])
    send_refs[2][...] = jnp.where(even, sides[3], sides[2])
    send_refs[3][...] = jnp.where(even, sides[2], sides[3])


def end_kernel(row_ref, state_ref, near_ref, *refs):
    in_refs, (place_ref, speed_ref) = refs[:4], refs[4:]
    side = lax.rem(lax.axis_index("mx"), 2)
    even = lax.rem(lax.axis_index("my"), 2)
    lists = row_ref[0, ROW_ELASTIC : ROW_ELASTIC + TILE, :]
    order = [
        jnp.where(side == 0, lists[5:6], lists[4:5]),
        jnp.where(side == 0, lists[4:5], lists[5:6]),
        jnp.where(even == 0, lists[7:8], lists[6:7]),
        jnp.where(even == 0, lists[6:7], lists[7:8]),
    ]
    total = near_ref[...] + faces([ref[...] for ref in in_refs], order)
    mass = row_ref[0, ROW_MASS : ROW_MASS + 1, :]
    speed = state_ref[4:7, :] + time_step * mass * total[0:3]
    speed_ref[...] = speed
    place_ref[...] = state_ref[0:3, :] + time_step * speed


def call(kernel, name, outs, scratch, *args, result=pltpu.VMEM, keep=True):
    return pl.pallas_call(
        kernel,
        name=name,
        out_shape=[result(shape, jnp.float32) for shape in outs],
        in_specs=[pl.BlockSpec(memory_space=pltpu.VMEM)] * len(args),
        out_specs=[pl.BlockSpec(memory_space=pltpu.VMEM)] * len(outs),
        scratch_shapes=[pltpu.VMEM(shape, jnp.float32) for shape in scratch],
    )(*[pltpu.with_memory_space_constraint(arg, pltpu.VMEM) if keep else arg for arg in args])


def swap(value, axis, first):
    size = lax.axis_size(axis)
    pairs = [(i, i + 1) for i in range(first, size - 1, 2)]
    return lax.ppermute(value, axis, pairs + [(j, i) for i, j in pairs])


def gather_row(record, axis):
    size = lax.axis_size(axis)
    held = record[None]
    step = size // 2
    while step:
        other = lax.ppermute(held, axis, [(i, i ^ step) for i in range(size)])
        held = jnp.concatenate([held, other], axis=0)
        step //= 2
    return held


def slot_of(me, device, size):
    apart = jnp.bitwise_xor(me, device)
    slot, step, place = 0, size // 2, 1
    while step:
        slot = slot + place * (lax.div(apart, step) & 1)
        step, place = step // 2, place * 2
    return slot


def body(
    positions, velocities, rest_positions, inverse_mass, element_nodes, modulus, stiffness, shared_lists, patch_nodes,
    patch_owner, pair_map,
):
    width = lax.axis_size("my")
    patches = patch_owner.shape[0]
    corners, elements = element_nodes.shape
    count = width * patches
    modulus, mass = modulus[None], inverse_mass[None]
    element_parts = (TILE * corners * elements // LANES, LANES)
    tile = (TILE, LANES)
    record, *held = call(
        pack_kernel,
        "pack",
        [(ROW_PATCH + 2 * patches, LANES), (3, LANES), (corners, elements), (1, elements), stiffness.shape],
        [element_parts],
        positions, velocities, rest_positions, mass, element_nodes, modulus, stiffness, shared_lists, patch_nodes,
        patch_owner[None], pair_map, keep=False,
    )
    row = gather_row(record, "my")
    total, pair, other, table = call(
        functools.partial(row_kernel, width, patches),
        "row",
        [(width, TILE, LANES), (width, 4, LANES), (width, 4, LANES), (6 * patches, LANES)],
        [(TILE * count, LANES)] * 2 + [(6 * count, LANES)] + [(2 * count, LANES)] * 2,
        row,
    )
    pair, other = swap(pair, "mx", 0), swap(other, "mx", 1)
    state, near, *sends = call(
        functools.partial(step_kernel, width, patches),
        "step",
        [tile] * 6,
        [(width, TILE, LANES), element_parts, (TILE * 2 * patches, LANES)],
        row, total, pair, other, table, *held,
    )
    ways = (("mx", 0), ("mx", 1), ("my", 0), ("my", 1))
    arrived = [swap(send, axis, first) for send, (axis, first) in zip(sends, ways)]
    return tuple(
        call(end_kernel, "end", [(3, LANES), (3, LANES)], [], row, state, near, *arrived, result=jax.ShapeDtypeStruct)
    )


def solution(mesh):
    in_specs = (
        P(None, ("mx", "my")),
        P(None, ("mx", "my")),
        P(None, ("mx", "my")),
        P(("mx", "my")),
        P(None, ("mx", "my")),
        P(("mx", "my")),
        P(),
        P(None, ("mx", "my")),
        P(("mx", "my"), None),
        P(("mx", "my")),
        P(("mx", "my"), None),
    )
    out_specs = (P(None, ("mx", "my")), P(None, ("mx", "my")))
    return jax.shard_map(body, mesh=mesh, in_specs=in_specs, out_specs=out_specs, check_vma=False)
```

```python
import functools

import jax
import jax.numpy as jnp
from jax import lax
from jax.experimental import pallas as pl
from jax.experimental.pallas import tpu as pltpu
from jax.sharding import PartitionSpec as P

STEPS = 2

time_step = 0.1
penalty = 4.0
damping = 0.5
contact_reach = 4.0
LANES = 128
TILE = 8
FINE = 32
VMEM_GRANT = 16 << 20
ROW_MASS, ROW_SPEED, ROW_OWNER, ROW_ELASTIC, ROW_LISTS, ROW_PATCH = 3, 4, 7, 8, 12, 16


def pick(rows, indices):
    return jnp.take_along_axis(rows, indices, axis=1)


def parted(indices):
    coarse = jnp.floor(indices * (1.0 / FINE))
    return coarse, indices - FINE * coarse


def put_parts(parts_ref, values, base=0):
    for c, value in enumerate(values):
        high = value.astype(jnp.bfloat16).astype(jnp.float32)
        rest = value - high
        for b in range(value.shape[0] // TILE):
            at = base + b * TILE * TILE
            parts_ref[at + c * TILE : at + (c + 1) * TILE, :] = high[b * TILE : (b + 1) * TILE]
            parts_ref[at + (4 + c) * TILE : at + (5 + c) * TILE, :] = rest[b * TILE : (b + 1) * TILE]


def get_parts(parts_ref, row):
    if isinstance(row, int):
        start = row // TILE * TILE * TILE + row % TILE
    else:
        start = lax.div(row, TILE) * (TILE * TILE) + lax.rem(row, TILE)
    return parts_ref[pl.ds(start, TILE, stride=TILE), :]


def scatter(entries):
    blocks = LANES // FINE
    total = jnp.zeros((blocks * TILE, FINE), jnp.float32)
    for coarse, fine, weights in entries:
        wide = weights.shape[1]
        shape = (blocks * TILE, wide)
        block = (lax.broadcasted_iota(jnp.int32, shape, 0) // TILE).astype(jnp.float32).astype(jnp.bfloat16)
        placed = jnp.where(
            jnp.broadcast_to(coarse, shape).astype(jnp.bfloat16) == block,
            jnp.concatenate([weights] * blocks, axis=0).astype(jnp.bfloat16),
            jnp.zeros(shape, jnp.bfloat16),
        )
        shape = (FINE, wide)
        node = lax.broadcasted_iota(jnp.int32, shape, 0).astype(jnp.float32).astype(jnp.bfloat16)
        hot = jnp.where(
            jnp.broadcast_to(fine, shape).astype(jnp.bfloat16) == node,
            jnp.ones(shape, jnp.bfloat16),
            jnp.zeros(shape, jnp.bfloat16),
        )
        total += lax.dot_general(placed, hot, (((1,), (1,)), ((), ())), preferred_element_type=jnp.float32)
    tile = jnp.concatenate([total[b * TILE : (b + 1) * TILE] for b in range(blocks)], axis=1)
    return tile + pltpu.roll(tile, 4, 0)


def joined(entries):
    return [
        tuple(jnp.concatenate([a, b], axis=1) for a, b in zip(*two)) for two in zip(entries[0::2], entries[1::2])
    ]


def tile_parts(tile):
    high = tile.astype(jnp.bfloat16).astype(jnp.float32)
    rest = pltpu.roll(tile - high, 4, 0)
    row = lax.broadcasted_iota(jnp.int32, tile.shape, 0)
    return jnp.where(row < 4, high, rest)


def product(left, right):
    def parts(x):
        high = x.astype(jnp.bfloat16)
        return high, (x - high.astype(jnp.float32)).astype(jnp.bfloat16)

    (lh, lr), (rh, rr) = parts(left), parts(right)
    return sum(jnp.dot(a, b, preferred_element_type=jnp.float32) for a, b in ((lh, rh), (lr, rh), (lh, rr)))


def elastic_entries(units, stiffness, parts_ref):
    local, moduli = [], []
    for place, rest, connect, modulus in units:
        moved = place - rest
        for corners, scale in zip(connect, modulus):
            local.append(
                jnp.concatenate(
                    [
                        pick(jnp.broadcast_to(moved[c : c + 1], corners.shape), corners.astype(jnp.int32))
                        for c in range(3)
                    ],
                    axis=0,
                )
            )
            moduli.append(scale)
    forces = -jnp.concatenate(moduli, axis=1) * product(stiffness, jnp.concatenate(local, axis=1))
    lists, at = [], 0
    for _, _, connect, _ in units:
        base, count = at, connect[0].shape[0]
        for k in range(len(connect)):
            span = slice((at + k) * LANES, (at + k + 1) * LANES)
            put_parts(
                parts_ref, [forces[c * count : (c + 1) * count, span] for c in range(3)], (at + k) * count * TILE
            )
        split = [parted(corners) for corners in connect]
        lists.append(
            [
                (
                    jnp.concatenate([coarse[a : a + 1] for coarse, _ in split], axis=1),
                    jnp.concatenate([fine[a : a + 1] for _, fine in split], axis=1),
                    jnp.concatenate([get_parts(parts_ref, (base + k) * count + a) for k in range(len(connect))], axis=1),
                )
                for a in range(count)
            ]
        )
        at += len(connect)
    return lists


def pair_forces(mine, partner):
    offset = [b - a for a, b in zip(mine[:3], partner[:3])]
    distance = offset[0] * offset[0] + offset[1] * offset[1] + offset[2] * offset[2]
    weight = jnp.exp(-distance / contact_reach)
    return [
        -penalty * weight * o + damping * weight * (b - a)
        for o, a, b in zip(offset, mine[3:], partner[3:])
    ]


def choose(rows, device):
    chosen = jnp.broadcast_to(rows[0], device.shape)
    for d, row in enumerate(rows[1:], 1):
        chosen = jnp.where(device == d, row, chosen)
    return chosen


def pack_kernel(
    place_ref, speed_ref, rest_ref, mass_ref, connect_ref, modulus_ref, stiff_ref, lists_ref, patch_ref, owner_ref,
    map_ref, out_ref, keep_ref, parts_ref,
):
    patches = patch_ref.shape[0]
    corners, elements = connect_ref.shape
    runs = [slice(k * LANES, (k + 1) * LANES) for k in range(elements // LANES)]
    connect = [connect_ref[:, run].astype(jnp.float32) for run in runs]
    modulus = [modulus_ref[:, run] for run in runs]
    (entries,) = elastic_entries([(place_ref[...], rest_ref[...], connect, modulus)], stiff_ref[...], parts_ref)
    keep_ref[...] = stiff_ref[...]
    out_ref[0:3, :] = place_ref[...]
    out_ref[ROW_MASS : ROW_MASS + 1, :] = mass_ref[...]
    out_ref[ROW_SPEED : ROW_SPEED + 3, :] = speed_ref[...]
    out_ref[ROW_OWNER : ROW_OWNER + 1, :] = jnp.zeros((1, LANES), jnp.float32)
    out_ref[ROW_OWNER : ROW_OWNER + 1, 0:patches] = owner_ref[...].astype(jnp.float32)
    out_ref[ROW_PATCH : ROW_PATCH + patches, :] = patch_ref[...].astype(jnp.float32)
    out_ref[ROW_PATCH + patches : ROW_PATCH + 2 * patches, :] = map_ref[...].astype(jnp.float32)
    base = ROW_PATCH + 2 * patches
    for k, run in enumerate(runs):
        out_ref[base + k * corners : base + (k + 1) * corners, :] = connect[k]
    last = base + len(runs) * corners
    out_ref[last : last + TILE, :] = jnp.zeros((TILE, LANES), jnp.float32)
    out_ref[last : last + 3, :] = rest_ref[...]
    for k, scale in enumerate(modulus):
        out_ref[last + 4 + k : last + 5 + k, :] = scale
    out_ref[ROW_ELASTIC : ROW_ELASTIC + TILE, :] = scatter(entries)
    out_ref[ROW_LISTS : ROW_LISTS + 4, :] = lists_ref[...].astype(jnp.float32)


def route(table, rows):
    return jnp.dot(table, rows.astype(jnp.bfloat16), preferred_element_type=jnp.float32)


def put_contact(width, patches, state, indices, back, parts_ref, back_ref):
    count = width * patches
    nodes, target, device = [part.astype(jnp.int32) for part in indices]
    mine, partner = [], []
    for c in (0, 1, 2, 4, 5, 6):
        rows = [tile[c : c + 1] for tile in state]
        own = jnp.concatenate([jnp.broadcast_to(row, (patches, LANES)) for row in rows], axis=0)
        mine.append(pick(own, nodes))
        partner.append(pick(choose(rows, device), target))
    forces = pair_forces(mine, partner)
    put_parts(parts_ref, forces)
    for c, force in enumerate(forces):
        high = force.astype(jnp.bfloat16).astype(jnp.float32)
        for g, part in ((c, high), (4 + c, force - high)):
            routed = -route(back, part)
            for b in range(count // TILE):
                at = b * TILE * TILE + g * TILE
                back_ref[at : at + TILE, :] = routed[b * TILE : (b + 1) * TILE]


def contact_entries(width, patches, u, coarse_ref, fine_ref, parts_ref, back_ref):
    entries = []
    for base, ref in ((0, parts_ref), (width * patches, back_ref)):
        for s in range(patches):
            at = u * patches + s
            entries.append((coarse_ref[pl.ds(base + at, 1), :], fine_ref[pl.ds(base + at, 1), :], get_parts(ref, at)))
    return joined(entries)


def each_unit(width, unit):
    if width <= 4:
        for u in range(width):
            unit(u)
    else:
        lax.fori_loop(0, width, lambda u, carry: (unit(u), carry)[1], 0)


def face_values(tile, row):
    return pick(tile, jnp.broadcast_to(row.astype(jnp.int32), tile.shape))


def row_kernel(
    width, patches, row_ref, total_ref, pair_ref, other_ref, idx_ref, link_ref, coarse_ref, fine_ref, parts_ref, back_ref
):
    me = lax.axis_index("my")
    side = lax.rem(lax.axis_index("mx"), 2)
    count = width * patches
    slot = [slot_of(me, u, width) for u in range(width)]
    state = [row_ref[slot[u], 0:TILE, :] for u in range(width)]
    nodes = jnp.concatenate([row_ref[slot[u], ROW_PATCH : ROW_PATCH + patches, :] for u in range(width)], axis=0)
    pairs = jnp.concatenate(
        [row_ref[slot[u], ROW_PATCH + patches : ROW_PATCH + 2 * patches, :] for u in range(width)], axis=0
    )
    lane = lax.broadcasted_iota(jnp.int32, (patches, LANES), 1)
    line = lax.broadcasted_iota(jnp.int32, (patches, LANES), 0)
    owner_col = jnp.concatenate(
        [
            jnp.sum(jnp.where(lane == line, state[u][ROW_OWNER : ROW_OWNER + 1], 0.0), axis=1, keepdims=True)
            for u in range(width)
        ],
        axis=0,
    )
    p = lax.broadcasted_iota(jnp.int32, (count, count), 0).astype(jnp.float32)
    q = lax.broadcasted_iota(jnp.int32, (count, count), 1).astype(jnp.float32)
    owner_row = jnp.sum(jnp.where(p == q, owner_col, 0.0), axis=0, keepdims=True)
    same = owner_col == owner_row
    after = jnp.min(jnp.where(same, jnp.where(q > p, q, q + count), 3.0 * count), axis=1, keepdims=True)
    after = jnp.where(after >= count, after - count, after)
    before = jnp.max(jnp.where(same, jnp.where(q < p, q + count, q), -1.0), axis=1, keepdims=True)
    before = jnp.where(before >= count, before - count, before)
    link = jnp.where(q == after, 1.0, 0.0).astype(jnp.bfloat16)
    back = jnp.where(q == before, 1.0, 0.0)
    link_ref[...] = back
    back = back.astype(jnp.bfloat16)
    target = pick(route(link, nodes), pairs.astype(jnp.int32))
    device = jnp.broadcast_to(jnp.floor(after / patches), (count, LANES))
    idx_ref[0:count, :] = nodes
    idx_ref[count : 2 * count, :] = target
    idx_ref[2 * count : 3 * count, :] = device
    coarse, fine = parted(jnp.concatenate([nodes, route(back, target)], axis=0))
    coarse_ref[...] = coarse
    fine_ref[...] = fine
    put_contact(width, patches, state, (nodes, target, device), back, parts_ref, back_ref)

    def unit(u):
        info = row_ref[slot_of(me, u, width), ROW_ELASTIC : ROW_ELASTIC + TILE, :]
        total = scatter(contact_entries(width, patches, u, coarse_ref, fine_ref, parts_ref, back_ref)) + info
        total_ref[u] = total
        low, high = face_values(total, info[4:5]), face_values(total, info[5:6])
        pair_ref[u] = jnp.where(side == 0, high, low)[0:4]
        other_ref[u] = jnp.where(side == 0, low, high)[0:4]

    each_unit(width, unit)


def faces(tiles, lists):
    return scatter(joined([(*parted(row), tile_parts(tile)) for row, tile in zip(lists, tiles)]))


def inside(axis):
    at, size = lax.axis_index(axis), lax.axis_size(axis)
    partner = at - 1 + 2 * lax.rem(at, 2)
    return jnp.logical_and(partner >= 0, partner < size)


def step_kernel(
    width, patches, corners, row_ref, total_ref, pair_ref, other_ref, idx_ref, link_ref, coarse_ref, fine_ref, stiff_ref,
    state_ref, near_ref, low_ref, high_ref, send_ref, far_ref, next_ref, element_ref, parts_ref, back_ref,
):
    me = lax.axis_index("my")
    side = lax.rem(lax.axis_index("mx"), 2)
    joins = inside("mx")
    count = width * patches
    blank = jnp.zeros((4, LANES), jnp.float32)

    def unit(u):
        info = row_ref[slot_of(me, u, width), 0 : 2 * TILE, :]
        lists = info[ROW_LISTS : ROW_LISTS + 4]
        down, up = jnp.maximum(u - 1, 0), jnp.minimum(u + 1, width - 1)
        low = face_values(total_ref[down], row_ref[slot_of(me, down, width), ROW_LISTS + 3 : ROW_LISTS + 4, :])
        high = face_values(total_ref[up], row_ref[slot_of(me, up, width), ROW_LISTS + 2 : ROW_LISTS + 3, :])
        tiles = [
            jnp.concatenate([pair_ref[u], blank], axis=0),
            jnp.where(joins, jnp.concatenate([other_ref[u], blank], axis=0), 0.0),
            jnp.where(u > 0, low, 0.0),
            jnp.where(u < width - 1, high, 0.0),
        ]
        near, far = jnp.where(side == 0, lists[1:2], lists[0:1]), jnp.where(side == 0, lists[0:1], lists[1:2])
        total = total_ref[u] + faces(tiles, [near, far, lists[2:3], lists[3:4]])
        speed = info[ROW_SPEED : ROW_SPEED + 3] + time_step * info[ROW_MASS : ROW_MASS + 1] * total[0:3]
        next_ref[u, 0:3, :] = info[0:3] + time_step * speed
        next_ref[u, 4:7, :] = speed

    each_unit(width, unit)
    state_ref[...] = next_ref[me]
    state = [next_ref[u] for u in range(width)]
    indices = [idx_ref[g * count : (g + 1) * count, :] for g in range(3)]
    put_contact(width, patches, state, indices, link_ref[...].astype(jnp.bfloat16), parts_ref, back_ref)
    around = [me, jnp.maximum(me - 1, 0), jnp.minimum(me + 1, width - 1)]
    base = ROW_PATCH + 2 * patches
    last = row_ref.shape[1] - TILE
    units = []
    for u in around:
        slot = slot_of(me, u, width)
        runs = (last - base) // corners
        connect = [row_ref[slot, base + k * corners : base + (k + 1) * corners, :] for k in range(runs)]
        tail = row_ref[slot, last : last + TILE, :]
        units.append((next_ref[u][0:3], tail[0:3], connect, [tail[4 + k : 5 + k] for k in range(runs)]))
    elastic = elastic_entries(units, stiff_ref[...], element_ref)
    totals = [
        scatter(entries + contact_entries(width, patches, u, coarse_ref, fine_ref, parts_ref, back_ref))
        for u, entries in zip(around, elastic)
    ]
    near_ref[...] = totals[0]
    low = face_values(totals[1], row_ref[slot_of(me, around[1], width), ROW_LISTS + 3 : ROW_LISTS + 4, :])
    high = face_values(totals[2], row_ref[slot_of(me, around[2], width), ROW_LISTS + 2 : ROW_LISTS + 3, :])
    low_ref[...] = jnp.where(me > 0, low, 0.0)
    high_ref[...] = jnp.where(me < width - 1, high, 0.0)
    lists = row_ref[0, ROW_LISTS : ROW_LISTS + 4, :]
    low, high = face_values(totals[0], lists[0:1]), face_values(totals[0], lists[1:2])
    send_ref[...] = jnp.where(side == 0, high, low)
    far_ref[...] = jnp.where(side == 0, low, high)


def end_kernel(row_ref, state_ref, near_ref, low_ref, high_ref, pair_ref, other_ref, place_ref, speed_ref):
    side = lax.rem(lax.axis_index("mx"), 2)
    info = row_ref[0, 0 : 2 * TILE, :]
    lists = info[ROW_LISTS : ROW_LISTS + 4]
    near, far = jnp.where(side == 0, lists[1:2], lists[0:1]), jnp.where(side == 0, lists[0:1], lists[1:2])
    tiles = [pair_ref[...], jnp.where(inside("mx"), other_ref[...], 0.0), low_ref[...], high_ref[...]]
    total = near_ref[...] + faces(tiles, [near, far, lists[2:3], lists[3:4]])
    speed = state_ref[4:7, :] + time_step * info[ROW_MASS : ROW_MASS + 1] * total[0:3]
    speed_ref[...] = speed
    place_ref[...] = state_ref[0:3, :] + time_step * speed


def call(kernel, name, outs, scratch, *args, result=pltpu.VMEM, keep=True):
    return pl.pallas_call(
        kernel,
        name=name,
        out_shape=[result(shape, jnp.float32) for shape in outs],
        in_specs=[pl.BlockSpec(memory_space=pltpu.VMEM)] * len(args),
        out_specs=[pl.BlockSpec(memory_space=pltpu.VMEM)] * len(outs),
        scratch_shapes=[pltpu.VMEM(shape, jnp.float32) for shape in scratch],
        compiler_params=pltpu.CompilerParams(vmem_limit_bytes=VMEM_GRANT),
    )(*[pltpu.with_memory_space_constraint(arg, pltpu.VMEM) if keep else arg for arg in args])


def swap(value, axis, first):
    size = lax.axis_size(axis)
    pairs = [(i, i + 1) for i in range(first, size - 1, 2)]
    if first and size % 2 == 0:
        pairs.append((0, size - 1))
    return lax.ppermute(value, axis, pairs + [(j, i) for i, j in pairs])


def gather_row(record, axis):
    size = lax.axis_size(axis)
    held = record[None]
    step = size // 2
    while step:
        other = lax.ppermute(held, axis, [(i, i ^ step) for i in range(size)])
        held = jnp.concatenate([held, other], axis=0)
        step //= 2
    return held


def slot_of(me, device, size):
    apart = jnp.bitwise_xor(me, device)
    slot, step, place = 0, size // 2, 1
    while step:
        slot = slot + place * (lax.div(apart, step) & 1)
        step, place = step // 2, place * 2
    return slot


def body(
    positions, velocities, rest_positions, inverse_mass, element_nodes, modulus, stiffness, shared_lists, patch_nodes,
    patch_owner, pair_map,
):
    width = lax.axis_size("my")
    patches = patch_owner.shape[0]
    corners, elements = element_nodes.shape
    count = width * patches
    modulus, mass = modulus[None], inverse_mass[None]
    runs = elements // LANES
    element_parts = (TILE * corners * runs, LANES)
    tile = (TILE, LANES)
    parts = (TILE * count, LANES)
    record, stiff = call(
        pack_kernel,
        "pack",
        [(ROW_PATCH + 2 * patches + runs * corners + TILE, LANES), stiffness.shape],
        [element_parts],
        positions, velocities, rest_positions, mass, element_nodes, modulus, stiffness, shared_lists, patch_nodes,
        patch_owner[None], pair_map, keep=False,
    )
    row = gather_row(record, "my")
    total, pair, other, *tables = call(
        functools.partial(row_kernel, width, patches),
        "row",
        [(width, TILE, LANES), (width, 4, LANES), (width, 4, LANES), (3 * count, LANES), (count, count)]
        + [(2 * count, LANES)] * 2,
        [parts, parts],
        row,
    )
    pair, other = swap(pair, "mx", 0), swap(other, "mx", 1)
    state, near, low, high, pair, other = call(
        functools.partial(step_kernel, width, patches, corners),
        "step",
        [tile] * 6,
        [(width, TILE, LANES), (3 * element_parts[0], LANES), parts, parts],
        row, total, pair, other, *tables, stiff,
    )
    pair, other = swap(pair, "mx", 0), swap(other, "mx", 1)
    outs = [(3, LANES), (3, LANES)]
    return tuple(
        call(end_kernel, "end", outs, [], row, state, near, low, high, pair, other, result=jax.ShapeDtypeStruct)
    )


def solution(mesh):
    in_specs = (
        P(None, ("mx", "my")),
        P(None, ("mx", "my")),
        P(None, ("mx", "my")),
        P(("mx", "my")),
        P(None, ("mx", "my")),
        P(("mx", "my")),
        P(),
        P(None, ("mx", "my")),
        P(("mx", "my"), None),
        P(("mx", "my")),
        P(("mx", "my"), None),
    )
    out_specs = (P(None, ("mx", "my")), P(None, ("mx", "my")))
    return jax.shard_map(body, mesh=mesh, in_specs=in_specs, out_specs=out_specs, check_vma=False)
```

```python
import functools

import jax
import jax.numpy as jnp
from jax import lax
from jax.experimental import pallas as pl
from jax.experimental.pallas import tpu as pltpu
from jax.sharding import PartitionSpec as P


time_step = 0.1
penalty = 4.0
damping = 0.5
contact_reach = 4.0
LANES = 128
TILE = 8
FINE = 32
VMEM_GRANT = 16 << 20
ROW_MASS, ROW_SPEED, ROW_OWNER, ROW_ELASTIC, ROW_LISTS, ROW_PATCH = 3, 4, 7, 8, 12, 16


def pick(rows, indices):
    return jnp.take_along_axis(rows, indices, axis=1)


def parted(indices):
    coarse = jnp.floor(indices * (1.0 / FINE))
    return coarse, indices - FINE * coarse


def put_parts(parts_ref, values, base=0):
    for c, value in enumerate(values):
        high = value.astype(jnp.bfloat16).astype(jnp.float32)
        rest = value - high
        for b in range(value.shape[0] // TILE):
            at = base + b * TILE * TILE
            parts_ref[at + c * TILE : at + (c + 1) * TILE, :] = high[b * TILE : (b + 1) * TILE]
            parts_ref[at + (4 + c) * TILE : at + (5 + c) * TILE, :] = rest[b * TILE : (b + 1) * TILE]


def get_parts(parts_ref, row):
    if isinstance(row, int):
        start = row // TILE * TILE * TILE + row % TILE
    else:
        start = lax.div(row, TILE) * (TILE * TILE) + lax.rem(row, TILE)
    return parts_ref[pl.ds(start, TILE, stride=TILE), :]


def scatter(entries, chains=2):
    blocks = LANES // FINE
    tiles = []
    for first in range(min(chains, len(entries))):
        total = jnp.zeros((blocks * TILE, FINE), jnp.float32)
        for coarse, fine, weights in entries[first::chains]:
            wide = weights.shape[1]
            shape = (blocks * TILE, wide)
            block = (lax.broadcasted_iota(jnp.int32, shape, 0) // TILE).astype(jnp.float32).astype(jnp.bfloat16)
            placed = jnp.where(
                jnp.broadcast_to(coarse, shape).astype(jnp.bfloat16) == block,
                jnp.concatenate([weights] * blocks, axis=0).astype(jnp.bfloat16),
                jnp.zeros(shape, jnp.bfloat16),
            )
            shape = (FINE, wide)
            node = lax.broadcasted_iota(jnp.int32, shape, 0).astype(jnp.float32).astype(jnp.bfloat16)
            hot = jnp.where(
                jnp.broadcast_to(fine, shape).astype(jnp.bfloat16) == node,
                jnp.ones(shape, jnp.bfloat16),
                jnp.zeros(shape, jnp.bfloat16),
            )
            total += lax.dot_general(placed, hot, (((1,), (1,)), ((), ())), preferred_element_type=jnp.float32)
        tile = jnp.concatenate([total[b * TILE : (b + 1) * TILE] for b in range(blocks)], axis=1)
        tiles.append(tile + pltpu.roll(tile, 4, 0))
    return sum(tiles[1:], tiles[0])


def joined(entries):
    return [
        tuple(jnp.concatenate([a, b], axis=1) for a, b in zip(*two)) for two in zip(entries[0::2], entries[1::2])
    ]


def tile_parts(tile):
    high = tile.astype(jnp.bfloat16).astype(jnp.float32)
    rest = pltpu.roll(tile - high, 4, 0)
    row = lax.broadcasted_iota(jnp.int32, tile.shape, 0)
    return jnp.where(row < 4, high, rest)


def product(left, right):
    def parts(x):
        high = x.astype(jnp.bfloat16)
        return high, (x - high.astype(jnp.float32)).astype(jnp.bfloat16)

    (lh, lr), (rh, rr) = parts(left), parts(right)
    return sum(jnp.dot(a, b, preferred_element_type=jnp.float32) for a, b in ((lh, rh), (lr, rh), (lh, rr)))


def elastic_entries(units, stiffness, parts_ref):
    local, moduli = [], []
    for place, rest, connect, modulus in units:
        moved = place - rest
        for corners, scale in zip(connect, modulus):
            local.append(
                jnp.concatenate(
                    [
                        pick(jnp.broadcast_to(moved[c : c + 1], corners.shape), corners.astype(jnp.int32))
                        for c in range(3)
                    ],
                    axis=0,
                )
            )
            moduli.append(scale)
    forces = -jnp.concatenate(moduli, axis=1) * product(stiffness, jnp.concatenate(local, axis=1))
    lists, at = [], 0
    for _, _, connect, _ in units:
        base, count = at, connect[0].shape[0]
        for k in range(len(connect)):
            span = slice((at + k) * LANES, (at + k + 1) * LANES)
            put_parts(
                parts_ref, [forces[c * count : (c + 1) * count, span] for c in range(3)], (at + k) * count * TILE
            )
        split = [parted(corners) for corners in connect]
        lists.append(
            [
                (
                    jnp.concatenate([coarse[a : a + 1] for coarse, _ in split], axis=1),
                    jnp.concatenate([fine[a : a + 1] for _, fine in split], axis=1),
                    jnp.concatenate([get_parts(parts_ref, (base + k) * count + a) for k in range(len(connect))], axis=1),
                )
                for a in range(count)
            ]
        )
        at += len(connect)
    return lists


def pair_forces(mine, partner):
    offset = [b - a for a, b in zip(mine[:3], partner[:3])]
    distance = offset[0] * offset[0] + offset[1] * offset[1] + offset[2] * offset[2]
    weight = jnp.exp(-distance / contact_reach)
    return [
        -penalty * weight * o + damping * weight * (b - a)
        for o, a, b in zip(offset, mine[3:], partner[3:])
    ]


def choose(rows, device):
    chosen = jnp.broadcast_to(rows[0], device.shape)
    for d, row in enumerate(rows[1:], 1):
        chosen = jnp.where(device == d, row, chosen)
    return chosen


def pack_kernel(
    place_ref, speed_ref, rest_ref, mass_ref, connect_ref, modulus_ref, stiff_ref, lists_ref, patch_ref, owner_ref,
    map_ref, out_ref, keep_ref, parts_ref,
):
    patches = patch_ref.shape[0]
    corners, elements = connect_ref.shape
    runs = [slice(k * LANES, (k + 1) * LANES) for k in range(elements // LANES)]
    connect = [connect_ref[:, run].astype(jnp.float32) for run in runs]
    modulus = [modulus_ref[:, run] for run in runs]
    (entries,) = elastic_entries([(place_ref[...], rest_ref[...], connect, modulus)], stiff_ref[...], parts_ref)
    keep_ref[...] = stiff_ref[...]
    out_ref[0:3, :] = place_ref[...]
    out_ref[ROW_MASS : ROW_MASS + 1, :] = mass_ref[...]
    out_ref[ROW_SPEED : ROW_SPEED + 3, :] = speed_ref[...]
    out_ref[ROW_OWNER : ROW_OWNER + 1, :] = jnp.zeros((1, LANES), jnp.float32)
    out_ref[ROW_OWNER : ROW_OWNER + 1, 0:patches] = owner_ref[...].astype(jnp.float32)
    out_ref[ROW_PATCH : ROW_PATCH + patches, :] = patch_ref[...].astype(jnp.float32)
    out_ref[ROW_PATCH + patches : ROW_PATCH + 2 * patches, :] = map_ref[...].astype(jnp.float32)
    base = ROW_PATCH + 2 * patches
    for k, run in enumerate(runs):
        out_ref[base + k * corners : base + (k + 1) * corners, :] = connect[k]
    last = base + len(runs) * corners
    out_ref[last : last + TILE, :] = jnp.zeros((TILE, LANES), jnp.float32)
    out_ref[last : last + 3, :] = rest_ref[...]
    for k, scale in enumerate(modulus):
        out_ref[last + 4 + k : last + 5 + k, :] = scale
    out_ref[ROW_ELASTIC : ROW_ELASTIC + TILE, :] = scatter(entries)
    out_ref[ROW_LISTS : ROW_LISTS + 4, :] = lists_ref[...].astype(jnp.float32)


def route(table, rows):
    return jnp.dot(table, rows.astype(jnp.bfloat16), preferred_element_type=jnp.float32)


def put_contact(width, patches, state, indices, back, parts_ref, back_ref):
    count = width * patches
    nodes, target, device = [part.astype(jnp.int32) for part in indices]
    mine, partner = [], []
    for c in (0, 1, 2, 4, 5, 6):
        rows = [tile[c : c + 1] for tile in state]
        own = jnp.concatenate([jnp.broadcast_to(row, (patches, LANES)) for row in rows], axis=0)
        mine.append(pick(own, nodes))
        partner.append(pick(choose(rows, device), target))
    forces = pair_forces(mine, partner)
    put_parts(parts_ref, forces)
    for c, force in enumerate(forces):
        high = force.astype(jnp.bfloat16).astype(jnp.float32)
        for g, part in ((c, high), (4 + c, force - high)):
            routed = -route(back, part)
            for b in range(count // TILE):
                at = b * TILE * TILE + g * TILE
                back_ref[at : at + TILE, :] = routed[b * TILE : (b + 1) * TILE]


def contact_entries(width, patches, u, coarse_ref, fine_ref, parts_ref, back_ref):
    entries = []
    for base, ref in ((0, parts_ref), (width * patches, back_ref)):
        for s in range(patches):
            at = u * patches + s
            entries.append((coarse_ref[pl.ds(base + at, 1), :], fine_ref[pl.ds(base + at, 1), :], get_parts(ref, at)))
    return joined(entries)


def each_unit(width, unit):
    if width <= 4:
        for u in range(width):
            unit(u)
    else:
        lax.fori_loop(0, width, lambda u, carry: (unit(u), carry)[1], 0)


def face_values(tile, row):
    return pick(tile, jnp.broadcast_to(row.astype(jnp.int32), tile.shape))


def row_kernel(
    width, patches, row_ref, total_ref, pair_ref, other_ref, idx_ref, link_ref, coarse_ref, fine_ref, parts_ref, back_ref
):
    me = lax.axis_index("my")
    side = lax.rem(lax.axis_index("mx"), 2)
    count = width * patches
    slot = [slot_of(me, u, width) for u in range(width)]
    state = [row_ref[slot[u], 0:TILE, :] for u in range(width)]
    nodes = jnp.concatenate([row_ref[slot[u], ROW_PATCH : ROW_PATCH + patches, :] for u in range(width)], axis=0)
    pairs = jnp.concatenate(
        [row_ref[slot[u], ROW_PATCH + patches : ROW_PATCH + 2 * patches, :] for u in range(width)], axis=0
    )
    lane = lax.broadcasted_iota(jnp.int32, (patches, LANES), 1)
    line = lax.broadcasted_iota(jnp.int32, (patches, LANES), 0)
    owner_col = jnp.concatenate(
        [
            jnp.sum(jnp.where(lane == line, state[u][ROW_OWNER : ROW_OWNER + 1], 0.0), axis=1, keepdims=True)
            for u in range(width)
        ],
        axis=0,
    )
    p = lax.broadcasted_iota(jnp.int32, (count, count), 0).astype(jnp.float32)
    q = lax.broadcasted_iota(jnp.int32, (count, count), 1).astype(jnp.float32)
    owner_row = jnp.sum(jnp.where(p == q, owner_col, 0.0), axis=0, keepdims=True)
    same = owner_col == owner_row
    after = jnp.min(jnp.where(same, jnp.where(q > p, q, q + count), 3.0 * count), axis=1, keepdims=True)
    after = jnp.where(after >= count, after - count, after)
    before = jnp.max(jnp.where(same, jnp.where(q < p, q + count, q), -1.0), axis=1, keepdims=True)
    before = jnp.where(before >= count, before - count, before)
    link = jnp.where(q == after, 1.0, 0.0).astype(jnp.bfloat16)
    back = jnp.where(q == before, 1.0, 0.0)
    link_ref[...] = back
    back = back.astype(jnp.bfloat16)
    target = pick(route(link, nodes), pairs.astype(jnp.int32))
    device = jnp.broadcast_to(jnp.floor(after / patches), (count, LANES))
    idx_ref[0:count, :] = nodes
    idx_ref[count : 2 * count, :] = target
    idx_ref[2 * count : 3 * count, :] = device
    coarse, fine = parted(jnp.concatenate([nodes, route(back, target)], axis=0))
    coarse_ref[...] = coarse
    fine_ref[...] = fine
    put_contact(width, patches, state, (nodes, target, device), back, parts_ref, back_ref)

    def unit(u):
        info = row_ref[slot_of(me, u, width), ROW_ELASTIC : ROW_ELASTIC + TILE, :]
        total = scatter(contact_entries(width, patches, u, coarse_ref, fine_ref, parts_ref, back_ref), 1) + info
        total_ref[u] = total
        low, high = face_values(total, info[4:5]), face_values(total, info[5:6])
        pair_ref[u] = jnp.where(side == 0, high, low)[0:4]
        other_ref[u] = jnp.where(side == 0, low, high)[0:4]

    each_unit(width, unit)


def faces(tiles, lists):
    return scatter(joined([(*parted(row), tile_parts(tile)) for row, tile in zip(lists, tiles)]))


def inside(axis):
    at, size = lax.axis_index(axis), lax.axis_size(axis)
    partner = at - 1 + 2 * lax.rem(at, 2)
    return jnp.logical_and(partner >= 0, partner < size)


def step_kernel(
    width, patches, corners, row_ref, total_ref, pair_ref, other_ref, idx_ref, link_ref, coarse_ref, fine_ref, stiff_ref,
    state_ref, near_ref, low_ref, high_ref, send_ref, far_ref, next_ref, element_ref, parts_ref, back_ref,
):
    me = lax.axis_index("my")
    side = lax.rem(lax.axis_index("mx"), 2)
    joins = inside("mx")
    count = width * patches
    blank = jnp.zeros((4, LANES), jnp.float32)

    def unit(u):
        info = row_ref[slot_of(me, u, width), 0 : 2 * TILE, :]
        lists = info[ROW_LISTS : ROW_LISTS + 4]
        down, up = jnp.maximum(u - 1, 0), jnp.minimum(u + 1, width - 1)
        low = face_values(total_ref[down], row_ref[slot_of(me, down, width), ROW_LISTS + 3 : ROW_LISTS + 4, :])
        high = face_values(total_ref[up], row_ref[slot_of(me, up, width), ROW_LISTS + 2 : ROW_LISTS + 3, :])
        tiles = [
            jnp.concatenate([pair_ref[u], blank], axis=0),
            jnp.where(joins, jnp.concatenate([other_ref[u], blank], axis=0), 0.0),
            jnp.where(u > 0, low, 0.0),
            jnp.where(u < width - 1, high, 0.0),
        ]
        near, far = jnp.where(side == 0, lists[1:2], lists[0:1]), jnp.where(side == 0, lists[0:1], lists[1:2])
        total = total_ref[u] + faces(tiles, [near, far, lists[2:3], lists[3:4]])
        speed = info[ROW_SPEED : ROW_SPEED + 3] + time_step * info[ROW_MASS : ROW_MASS + 1] * total[0:3]
        next_ref[u, 0:3, :] = info[0:3] + time_step * speed
        next_ref[u, 4:7, :] = speed

    each_unit(width, unit)
    state_ref[...] = next_ref[me]
    state = [next_ref[u] for u in range(width)]
    around = [me, jnp.maximum(me - 1, 0), jnp.minimum(me + 1, width - 1)]
    base = ROW_PATCH + 2 * patches
    last = row_ref.shape[1] - TILE
    units = []
    for u in around:
        slot = slot_of(me, u, width)
        runs = (last - base) // corners
        connect = [row_ref[slot, base + k * corners : base + (k + 1) * corners, :] for k in range(runs)]
        tail = row_ref[slot, last : last + TILE, :]
        units.append((next_ref[u][0:3], tail[0:3], connect, [tail[4 + k : 5 + k] for k in range(runs)]))
    elastic = elastic_entries(units, stiff_ref[...], element_ref)
    indices = [idx_ref[g * count : (g + 1) * count, :] for g in range(3)]
    put_contact(width, patches, state, indices, link_ref[...].astype(jnp.bfloat16), parts_ref, back_ref)
    totals = [
        scatter(entries + contact_entries(width, patches, u, coarse_ref, fine_ref, parts_ref, back_ref))
        for u, entries in zip(around, elastic)
    ]
    near_ref[...] = totals[0]
    low = face_values(totals[1], row_ref[slot_of(me, around[1], width), ROW_LISTS + 3 : ROW_LISTS + 4, :])
    high = face_values(totals[2], row_ref[slot_of(me, around[2], width), ROW_LISTS + 2 : ROW_LISTS + 3, :])
    low_ref[...] = jnp.where(me > 0, low, 0.0)
    high_ref[...] = jnp.where(me < width - 1, high, 0.0)
    lists = row_ref[0, ROW_LISTS : ROW_LISTS + 4, :]
    low, high = face_values(totals[0], lists[0:1]), face_values(totals[0], lists[1:2])
    send_ref[...] = jnp.where(side == 0, high, low)
    far_ref[...] = jnp.where(side == 0, low, high)


def end_kernel(row_ref, state_ref, near_ref, low_ref, high_ref, pair_ref, other_ref, place_ref, speed_ref):
    side = lax.rem(lax.axis_index("mx"), 2)
    info = row_ref[0, 0 : 2 * TILE, :]
    lists = info[ROW_LISTS : ROW_LISTS + 4]
    near, far = jnp.where(side == 0, lists[1:2], lists[0:1]), jnp.where(side == 0, lists[0:1], lists[1:2])
    tiles = [pair_ref[...], jnp.where(inside("mx"), other_ref[...], 0.0), low_ref[...], high_ref[...]]
    total = near_ref[...] + faces(tiles, [near, far, lists[2:3], lists[3:4]])
    speed = state_ref[4:7, :] + time_step * info[ROW_MASS : ROW_MASS + 1] * total[0:3]
    speed_ref[...] = speed
    place_ref[...] = state_ref[0:3, :] + time_step * speed


def call(kernel, outs, scratch, *args, result=pltpu.VMEM, keep=True):
    return pl.pallas_call(
        kernel,
        out_shape=[result(shape, jnp.float32) for shape in outs],
        in_specs=[pl.BlockSpec(memory_space=pltpu.VMEM)] * len(args),
        out_specs=[pl.BlockSpec(memory_space=pltpu.VMEM)] * len(outs),
        scratch_shapes=[pltpu.VMEM(shape, jnp.float32) for shape in scratch],
        compiler_params=pltpu.CompilerParams(vmem_limit_bytes=VMEM_GRANT if keep else None),
    )(*[pltpu.with_memory_space_constraint(arg, pltpu.VMEM) if keep else arg for arg in args])


def swap(value, axis, first, other):
    size, depth = lax.axis_size(axis), lax.axis_size(other)
    pairs = []
    for i in range(size):
        partner = i + 1 - 2 * ((i - first) % 2)
        for k in range(depth):
            if 0 <= partner < size:
                pairs.append((i * depth + k, partner * depth + k))
            elif depth % 2 == 0:
                pairs.append((i * depth + k, i * depth + (k ^ 1)))
    return lax.ppermute(value, (axis, other), pairs)


def both(pair, other):
    other = swap(other, "mx", 1, "my")
    pair = swap(pair, "mx", 0, "my")
    return pair, other


def gather_row(record, axis):
    size = lax.axis_size(axis)
    held = record[None]
    step = size // 2
    while step:
        other = lax.ppermute(held, axis, [(i, i ^ step) for i in range(size)])
        held = jnp.concatenate([held, other], axis=0)
        step //= 2
    return held


def slot_of(me, device, size):
    apart = jnp.bitwise_xor(me, device)
    slot, step, place = 0, size // 2, 1
    while step:
        slot = slot + place * (lax.div(apart, step) & 1)
        step, place = step // 2, place * 2
    return slot


def body(
    positions, velocities, rest_positions, inverse_mass, element_nodes, modulus, stiffness, shared_lists, patch_nodes,
    patch_owner, pair_map,
):
    width = lax.axis_size("my")
    patches = patch_owner.shape[0]
    corners, elements = element_nodes.shape
    count = width * patches
    modulus, mass = modulus[None], inverse_mass[None]
    runs = elements // LANES
    element_parts = (TILE * corners * runs, LANES)
    tile = (TILE, LANES)
    parts = (TILE * count, LANES)
    record, stiff = call(
        pack_kernel,
        [(ROW_PATCH + 2 * patches + runs * corners + TILE, LANES), stiffness.shape],
        [element_parts],
        positions, velocities, rest_positions, mass, element_nodes, modulus, stiffness, shared_lists, patch_nodes,
        patch_owner[None], pair_map, keep=False,
    )
    row = gather_row(record, "my")
    total, pair, other, *tables = call(
        functools.partial(row_kernel, width, patches),
        [(width, TILE, LANES), (width, 4, LANES), (width, 4, LANES), (3 * count, LANES), (count, count)]
        + [(2 * count, LANES)] * 2,
        [parts, parts],
        row,
    )
    pair, other = both(pair, other)
    state, near, low, high, pair, other = call(
        functools.partial(step_kernel, width, patches, corners),
        [tile] * 6,
        [(width, TILE, LANES), (3 * element_parts[0], LANES), parts, parts],
        row, total, pair, other, *tables, stiff,
    )
    pair, other = both(pair, other)
    outs = [(3, LANES), (3, LANES)]
    return tuple(call(end_kernel, outs, [], row, state, near, low, high, pair, other, result=jax.ShapeDtypeStruct))


def solution(mesh):
    in_specs = (
        P(None, ("mx", "my")),
        P(None, ("mx", "my")),
        P(None, ("mx", "my")),
        P(("mx", "my")),
        P(None, ("mx", "my")),
        P(("mx", "my")),
        P(),
        P(None, ("mx", "my")),
        P(("mx", "my"), None),
        P(("mx", "my")),
        P(("mx", "my"), None),
    )
    out_specs = (P(None, ("mx", "my")), P(None, ("mx", "my")))
    return jax.shard_map(body, mesh=mesh, in_specs=in_specs, out_specs=out_specs, check_vma=False)
```

```python
import functools

import jax
import jax.numpy as jnp
from jax import lax
from jax.experimental import pallas as pl
from jax.experimental.pallas import tpu as pltpu
from jax.sharding import PartitionSpec as P


time_step = 0.1
penalty = 4.0
damping = 0.5
contact_reach = 4.0
LANES = 128
TILE = 8
FINE = 32
VMEM_GRANT = 16 << 20
ROW_MASS, ROW_SPEED, ROW_OWNER, ROW_ELASTIC, ROW_LISTS, ROW_PATCH = 3, 4, 7, 8, 12, 16


def pick(rows, indices):
    return jnp.take_along_axis(rows, indices, axis=1)


def parted(indices):
    coarse = jnp.floor(indices * (1.0 / FINE))
    return coarse, indices - FINE * coarse


def put_parts(parts_ref, values, base=0):
    for c, value in enumerate(values):
        high = value.astype(jnp.bfloat16).astype(jnp.float32)
        rest = value - high
        for b in range(value.shape[0] // TILE):
            at = base + b * TILE * TILE
            parts_ref[at + c * TILE : at + (c + 1) * TILE, :] = high[b * TILE : (b + 1) * TILE]
            parts_ref[at + (4 + c) * TILE : at + (5 + c) * TILE, :] = rest[b * TILE : (b + 1) * TILE]


def get_parts(parts_ref, row):
    if isinstance(row, int):
        start = row // TILE * TILE * TILE + row % TILE
    else:
        start = lax.div(row, TILE) * (TILE * TILE) + lax.rem(row, TILE)
    return parts_ref[pl.ds(start, TILE, stride=TILE), :]


def scatter(entries, chains=2):
    blocks = LANES // FINE
    tiles = []
    for first in range(min(chains, len(entries))):
        total = jnp.zeros((blocks * TILE, FINE), jnp.float32)
        for coarse, fine, weights in entries[first::chains]:
            wide = weights.shape[1]
            shape = (blocks * TILE, wide)
            block = (lax.broadcasted_iota(jnp.int32, shape, 0) // TILE).astype(jnp.float32).astype(jnp.bfloat16)
            placed = jnp.where(
                jnp.broadcast_to(coarse, shape).astype(jnp.bfloat16) == block,
                jnp.concatenate([weights] * blocks, axis=0).astype(jnp.bfloat16),
                jnp.zeros(shape, jnp.bfloat16),
            )
            shape = (FINE, wide)
            node = lax.broadcasted_iota(jnp.int32, shape, 0).astype(jnp.float32).astype(jnp.bfloat16)
            hot = jnp.where(
                jnp.broadcast_to(fine, shape).astype(jnp.bfloat16) == node,
                jnp.ones(shape, jnp.bfloat16),
                jnp.zeros(shape, jnp.bfloat16),
            )
            total += lax.dot_general(placed, hot, (((1,), (1,)), ((), ())), preferred_element_type=jnp.float32)
        tile = jnp.concatenate([total[b * TILE : (b + 1) * TILE] for b in range(blocks)], axis=1)
        tiles.append(tile + pltpu.roll(tile, 4, 0))
    return sum(tiles[1:], tiles[0])


def joined(entries):
    return [
        tuple(jnp.concatenate([a, b], axis=1) for a, b in zip(*two)) for two in zip(entries[0::2], entries[1::2])
    ]


def tile_parts(tile):
    high = tile.astype(jnp.bfloat16).astype(jnp.float32)
    rest = pltpu.roll(tile - high, 4, 0)
    row = lax.broadcasted_iota(jnp.int32, tile.shape, 0)
    return jnp.where(row < 4, high, rest)


def product(left, right):
    def parts(x):
        high = x.astype(jnp.bfloat16)
        return high, (x - high.astype(jnp.float32)).astype(jnp.bfloat16)

    (lh, lr), (rh, rr) = parts(left), parts(right)
    return sum(jnp.dot(a, b, preferred_element_type=jnp.float32) for a, b in ((lh, rh), (lr, rh), (lh, rr)))


def elastic_entries(units, stiffness, parts_ref):
    local, moduli = [], []
    for place, rest, connect, modulus in units:
        moved = place - rest
        for corners, scale in zip(connect, modulus):
            local.append(
                jnp.concatenate(
                    [
                        pick(jnp.broadcast_to(moved[c : c + 1], corners.shape), corners.astype(jnp.int32))
                        for c in range(3)
                    ],
                    axis=0,
                )
            )
            moduli.append(scale)
    forces = -jnp.concatenate(moduli, axis=1) * product(stiffness, jnp.concatenate(local, axis=1))
    lists, at = [], 0
    for _, _, connect, _ in units:
        base, count = at, connect[0].shape[0]
        for k in range(len(connect)):
            span = slice((at + k) * LANES, (at + k + 1) * LANES)
            put_parts(
                parts_ref, [forces[c * count : (c + 1) * count, span] for c in range(3)], (at + k) * count * TILE
            )
        split = [parted(corners) for corners in connect]
        lists.append(
            [
                (
                    jnp.concatenate([coarse[a : a + 1] for coarse, _ in split], axis=1),
                    jnp.concatenate([fine[a : a + 1] for _, fine in split], axis=1),
                    jnp.concatenate([get_parts(parts_ref, (base + k) * count + a) for k in range(len(connect))], axis=1),
                )
                for a in range(count)
            ]
        )
        at += len(connect)
    return lists


def pair_forces(mine, partner):
    offset = [b - a for a, b in zip(mine[:3], partner[:3])]
    distance = offset[0] * offset[0] + offset[1] * offset[1] + offset[2] * offset[2]
    weight = jnp.exp(-distance / contact_reach)
    return [
        -penalty * weight * o + damping * weight * (b - a)
        for o, a, b in zip(offset, mine[3:], partner[3:])
    ]


def choose(rows, device):
    chosen = jnp.broadcast_to(rows[0], device.shape)
    for d, row in enumerate(rows[1:], 1):
        chosen = jnp.where(device == d, row, chosen)
    return chosen


def pack_kernel(
    place_ref, speed_ref, rest_ref, mass_ref, connect_ref, modulus_ref, stiff_ref, lists_ref, patch_ref, owner_ref,
    map_ref, out_ref, keep_ref, parts_ref,
):
    patches = patch_ref.shape[0]
    corners, elements = connect_ref.shape
    runs = [slice(k * LANES, (k + 1) * LANES) for k in range(elements // LANES)]
    connect = [connect_ref[:, run].astype(jnp.float32) for run in runs]
    modulus = [modulus_ref[:, run] for run in runs]
    (entries,) = elastic_entries([(place_ref[...], rest_ref[...], connect, modulus)], stiff_ref[...], parts_ref)
    keep_ref[...] = stiff_ref[...]
    out_ref[0:3, :] = place_ref[...]
    out_ref[ROW_MASS : ROW_MASS + 1, :] = mass_ref[...]
    out_ref[ROW_SPEED : ROW_SPEED + 3, :] = speed_ref[...]
    out_ref[ROW_OWNER : ROW_OWNER + 1, :] = jnp.zeros((1, LANES), jnp.float32)
    out_ref[ROW_OWNER : ROW_OWNER + 1, 0:patches] = owner_ref[...].astype(jnp.float32)
    out_ref[ROW_PATCH : ROW_PATCH + patches, :] = patch_ref[...].astype(jnp.float32)
    out_ref[ROW_PATCH + patches : ROW_PATCH + 2 * patches, :] = map_ref[...].astype(jnp.float32)
    base = ROW_PATCH + 2 * patches
    for k, run in enumerate(runs):
        out_ref[base + k * corners : base + (k + 1) * corners, :] = connect[k]
    last = base + len(runs) * corners
    out_ref[last : last + TILE, :] = jnp.zeros((TILE, LANES), jnp.float32)
    out_ref[last : last + 3, :] = rest_ref[...]
    for k, scale in enumerate(modulus):
        out_ref[last + 4 + k : last + 5 + k, :] = scale
    out_ref[ROW_ELASTIC : ROW_ELASTIC + TILE, :] = scatter(entries)
    out_ref[ROW_LISTS : ROW_LISTS + 4, :] = lists_ref[...].astype(jnp.float32)


def route(table, rows):
    return jnp.dot(table, rows.astype(jnp.bfloat16), preferred_element_type=jnp.float32)


def put_contact(width, patches, state, indices, back, parts_ref, back_ref):
    count = width * patches
    nodes, target, device = [part.astype(jnp.int32) for part in indices]
    mine, partner = [], []
    for c in (0, 1, 2, 4, 5, 6):
        rows = [tile[c : c + 1] for tile in state]
        own = jnp.concatenate([jnp.broadcast_to(row, (patches, LANES)) for row in rows], axis=0)
        mine.append(pick(own, nodes))
        partner.append(pick(choose(rows, device), target))
    forces = pair_forces(mine, partner)
    put_parts(parts_ref, forces)
    for c, force in enumerate(forces):
        high = force.astype(jnp.bfloat16).astype(jnp.float32)
        for g, part in ((c, high), (4 + c, force - high)):
            routed = -route(back, part)
            for b in range(count // TILE):
                at = b * TILE * TILE + g * TILE
                back_ref[at : at + TILE, :] = routed[b * TILE : (b + 1) * TILE]


def contact_entries(width, patches, u, coarse_ref, fine_ref, parts_ref, back_ref):
    entries = []
    for base, ref in ((0, parts_ref), (width * patches, back_ref)):
        for s in range(patches):
            at = u * patches + s
            entries.append((coarse_ref[pl.ds(base + at, 1), :], fine_ref[pl.ds(base + at, 1), :], get_parts(ref, at)))
    return joined(entries)


def each_unit(width, unit):
    if width <= 4:
        for u in range(width):
            unit(u)
    else:
        lax.fori_loop(0, width, lambda u, carry: (unit(u), carry)[1], 0)


def face_values(tile, row):
    return pick(tile, jnp.broadcast_to(row.astype(jnp.int32), tile.shape))


def row_kernel(width, patches, where, *refs):
    total_ref, pair_ref, other_ref, keep_ref, idx_ref, link_ref, coarse_ref, fine_ref, parts_ref, back_ref = refs[-10:]
    me = lax.axis_index("my")
    side = lax.rem(lax.axis_index("mx"), 2)
    count = width * patches
    record = [refs[piece].at[place] for piece, place in where]
    state = [ref[0:TILE, :] for ref in record]
    nodes = jnp.concatenate([ref[ROW_PATCH : ROW_PATCH + patches, :] for ref in record], axis=0)
    pairs = jnp.concatenate([ref[ROW_PATCH + patches : ROW_PATCH + 2 * patches, :] for ref in record], axis=0)
    for s, ref in enumerate(record):
        keep_ref[s, 0:ROW_PATCH, :] = ref[0:ROW_PATCH, :]
        keep_ref[s, ROW_PATCH:, :] = ref[ROW_PATCH + 2 * patches :, :]
    lane = lax.broadcasted_iota(jnp.int32, (patches, LANES), 1)
    line = lax.broadcasted_iota(jnp.int32, (patches, LANES), 0)
    owner_col = jnp.concatenate(
        [
            jnp.sum(jnp.where(lane == line, state[u][ROW_OWNER : ROW_OWNER + 1], 0.0), axis=1, keepdims=True)
            for u in range(width)
        ],
        axis=0,
    )
    row, col = [lax.broadcasted_iota(jnp.int32, (count, count), axis) for axis in (0, 1)]
    owner_row = jnp.sum(jnp.where(row == col, owner_col, 0.0), axis=0, keepdims=True)
    p, q = [(((at // patches) ^ me) * patches + at % patches).astype(jnp.float32) for at in (row, col)]
    same = owner_col == owner_row
    after = jnp.min(jnp.where(same, jnp.where(q > p, q, q + count), 3.0 * count), axis=1, keepdims=True)
    after = jnp.where(after >= count, after - count, after)
    before = jnp.max(jnp.where(same, jnp.where(q < p, q + count, q), -1.0), axis=1, keepdims=True)
    before = jnp.where(before >= count, before - count, before)
    link = jnp.where(q == after, 1.0, 0.0).astype(jnp.bfloat16)
    back = jnp.where(q == before, 1.0, 0.0)
    link_ref[...] = back
    back = back.astype(jnp.bfloat16)
    target = pick(route(link, nodes), pairs.astype(jnp.int32))
    device = jnp.broadcast_to(jnp.floor(after / patches).astype(jnp.int32) ^ me, (count, LANES)).astype(jnp.float32)
    idx_ref[0:count, :] = nodes
    idx_ref[count : 2 * count, :] = target
    idx_ref[2 * count : 3 * count, :] = device
    coarse, fine = parted(jnp.concatenate([nodes, route(back, target)], axis=0))
    coarse_ref[...] = coarse
    fine_ref[...] = fine
    put_contact(width, patches, state, (nodes, target, device), back, parts_ref, back_ref)

    def unit(u):
        info = keep_ref[u, ROW_ELASTIC : ROW_ELASTIC + TILE, :]
        total = scatter(contact_entries(width, patches, u, coarse_ref, fine_ref, parts_ref, back_ref), 1) + info
        total_ref[u] = total
        low, high = face_values(total, info[4:5]), face_values(total, info[5:6])
        pair_ref[u] = jnp.where(side == 0, high, low)[0:4]
        other_ref[u] = jnp.where(side == 0, low, high)[0:4]

    each_unit(width, unit)


def faces(tiles, lists):
    return scatter(joined([(*parted(row), tile_parts(tile)) for row, tile in zip(lists, tiles)]))


def inside(axis):
    at, size = lax.axis_index(axis), lax.axis_size(axis)
    partner = at - 1 + 2 * lax.rem(at, 2)
    return jnp.logical_and(partner >= 0, partner < size)


def mid_kernel(width, keep_ref, total_ref, base_ref):
    me = lax.axis_index("my")

    def unit(s):
        info = keep_ref[s, 0 : 2 * TILE, :]
        u = me ^ s
        down, up = jnp.maximum(u - 1, 0) ^ me, jnp.minimum(u + 1, width - 1) ^ me
        low = face_values(total_ref[down], keep_ref[down, ROW_LISTS + 3 : ROW_LISTS + 4, :])
        high = face_values(total_ref[up], keep_ref[up, ROW_LISTS + 2 : ROW_LISTS + 3, :])
        tiles = [jnp.where(u > 0, low, 0.0), jnp.where(u < width - 1, high, 0.0)]
        total = total_ref[s] + faces(tiles, [info[ROW_LISTS + 2 : ROW_LISTS + 3], info[ROW_LISTS + 3 : ROW_LISTS + 4]])
        mass = info[ROW_MASS : ROW_MASS + 1]
        base_ref[s, 0:4, :] = info[0:4]
        base_ref[s, 4:7, :] = info[ROW_SPEED : ROW_SPEED + 3] + time_step * mass * total[0:3]

    each_unit(width, unit)


def mx_faces(lists, pair, other):
    side = lax.rem(lax.axis_index("mx"), 2)
    near, far = jnp.where(side == 0, lists[1:2], lists[0:1]), jnp.where(side == 0, lists[0:1], lists[1:2])
    return faces([pair, jnp.where(inside("mx"), other, 0.0)], [near, far])


def elements_of(keep_ref, next_ref, s, corners):
    last = keep_ref.shape[1] - TILE
    runs = (last - ROW_PATCH) // corners
    connect = [keep_ref[s, ROW_PATCH + k * corners : ROW_PATCH + (k + 1) * corners, :] for k in range(runs)]
    tail = keep_ref[s, last : last + TILE, :]
    return next_ref[s][0:3], tail[0:3], connect, [tail[4 + k : 5 + k] for k in range(runs)]


def step_kernel(
    width, patches, corners, keep_ref, base_ref, pair_ref, other_ref, idx_ref, link_ref, coarse_ref, fine_ref, stiff_ref,
    next_ref, near_ref, send_ref, far_ref, parts_ref, back_ref, element_ref,
):
    side = lax.rem(lax.axis_index("mx"), 2)
    count = width * patches
    blank = jnp.zeros((4, LANES), jnp.float32)

    def unit(s):
        base = base_ref[s]
        lists = keep_ref[s, ROW_LISTS : ROW_LISTS + 4, :]
        pair, other = [jnp.concatenate([ref[s], blank], axis=0) for ref in (pair_ref, other_ref)]
        speed = base[4:7] + time_step * base[3:4] * mx_faces(lists, pair, other)[0:3]
        next_ref[s, 0:3, :] = base[0:3] + time_step * speed
        next_ref[s, 4:7, :] = speed

    each_unit(width, unit)
    (elastic,) = elastic_entries([elements_of(keep_ref, next_ref, 0, corners)], stiff_ref[...], element_ref)
    state = [next_ref[s] for s in range(width)]
    indices = [idx_ref[g * count : (g + 1) * count, :] for g in range(3)]
    put_contact(width, patches, state, indices, link_ref[...].astype(jnp.bfloat16), parts_ref, back_ref)
    total = scatter(elastic + contact_entries(width, patches, 0, coarse_ref, fine_ref, parts_ref, back_ref))
    near_ref[...] = total
    lists = keep_ref[0, ROW_LISTS : ROW_LISTS + 4, :]
    low, high = face_values(total, lists[0:1]), face_values(total, lists[1:2])
    send_ref[...] = jnp.where(side == 0, high, low)
    far_ref[...] = jnp.where(side == 0, low, high)


def spare_kernel(
    width, patches, corners, keep_ref, next_ref, near_ref, coarse_ref, fine_ref, parts_ref, back_ref, stiff_ref,
    total_ref, element_ref,
):
    me = lax.axis_index("my")
    around = [jnp.maximum(me - 1, 0) ^ me, jnp.minimum(me + 1, width - 1) ^ me]
    elastic = elastic_entries([elements_of(keep_ref, next_ref, s, corners) for s in around], stiff_ref[...], element_ref)
    below, above = [
        scatter(entries + contact_entries(width, patches, s, coarse_ref, fine_ref, parts_ref, back_ref), 1)
        for s, entries in zip(around, elastic)
    ]
    low = face_values(below, keep_ref[around[0], ROW_LISTS + 3 : ROW_LISTS + 4, :])
    high = face_values(above, keep_ref[around[1], ROW_LISTS + 2 : ROW_LISTS + 3, :])
    lists = keep_ref[0, ROW_LISTS : ROW_LISTS + 4, :]
    tiles = [jnp.where(me > 0, low, 0.0), jnp.where(me < width - 1, high, 0.0)]
    total_ref[...] = near_ref[...] + faces(tiles, [lists[2:3], lists[3:4]])


def end_kernel(keep_ref, next_ref, total_ref, pair_ref, other_ref, place_ref, speed_ref):
    lists = keep_ref[0, ROW_LISTS : ROW_LISTS + 4, :]
    total = total_ref[...] + mx_faces(lists, pair_ref[...], other_ref[...])
    speed = next_ref[0, 4:7, :] + time_step * keep_ref[0, ROW_MASS : ROW_MASS + 1, :] * total[0:3]
    speed_ref[...] = speed
    place_ref[...] = next_ref[0, 0:3, :] + time_step * speed


def call(kernel, outs, scratch, *args, result=pltpu.VMEM, placed=True):
    return pl.pallas_call(
        kernel,
        out_shape=[result(shape, jnp.float32) for shape in outs],
        in_specs=[pl.BlockSpec(memory_space=pltpu.VMEM)] * len(args),
        out_specs=[pl.BlockSpec(memory_space=pltpu.VMEM)] * len(outs),
        scratch_shapes=[pltpu.VMEM(shape, jnp.float32) for shape in scratch],
        compiler_params=pltpu.CompilerParams(vmem_limit_bytes=VMEM_GRANT if placed else None),
    )(*[pltpu.with_memory_space_constraint(arg, pltpu.VMEM) if placed else arg for arg in args])


def swap(value, axis, first, other):
    size, depth = lax.axis_size(axis), lax.axis_size(other)
    pairs = []
    for i in range(size):
        partner = i + 1 - 2 * ((i - first) % 2)
        for k in range(depth):
            if 0 <= partner < size:
                pairs.append((i * depth + k, partner * depth + k))
            elif depth % 2 == 0:
                pairs.append((i * depth + k, i * depth + (k ^ 1)))
    return lax.ppermute(value, (axis, other), pairs)


def both(pair, other):
    other = swap(other, "mx", 1, "my")
    pair = swap(pair, "mx", 0, "my")
    return pair, other


def gather_row(record, axis):
    size = lax.axis_size(axis)
    steps = [size >> k for k in range(1, size.bit_length())]

    def exchange(value, step):
        return lax.ppermute(value, axis, [(i, i ^ step) for i in range(size)])

    direct = []
    for step in steps:
        direct.append(exchange(record[None], step))
    pieces, slots = [record[None]], [[0]]
    for step, near in zip(steps, direct):
        far, far_slots = pieces[1:], [s ^ step for held in slots[1:] for s in held]
        pieces, slots = pieces + [near], slots + [[step]]
        if far:
            pieces.append(exchange(far[0] if len(far) == 1 else jnp.concatenate(far, axis=0), step))
            slots.append(far_slots)
    where = {s: (n, k) for n, held in enumerate(slots) for k, s in enumerate(held)}
    return pieces, [where[s] for s in range(size)]


def body(
    positions, velocities, rest_positions, inverse_mass, element_nodes, modulus, stiffness, shared_lists, patch_nodes,
    patch_owner, pair_map,
):
    width = lax.axis_size("my")
    patches = patch_owner.shape[0]
    corners, elements = element_nodes.shape
    count = width * patches
    modulus, mass = modulus[None], inverse_mass[None]
    runs = elements // LANES
    element_parts = (TILE * corners * runs, LANES)
    tile = (TILE, LANES)
    parts = (TILE * count, LANES)
    record, stiff = call(
        pack_kernel,
        [(ROW_PATCH + 2 * patches + runs * corners + TILE, LANES), stiffness.shape],
        [element_parts],
        positions, velocities, rest_positions, mass, element_nodes, modulus, stiffness, shared_lists, patch_nodes,
        patch_owner[None], pair_map, placed=False,
    )
    pieces, where = gather_row(record, "my")
    kept = (width, record.shape[0] - 2 * patches, LANES)
    total, pair, other, keep, indices, link, *spots = call(
        functools.partial(row_kernel, width, patches, where),
        [(width, TILE, LANES), (width, 4, LANES), (width, 4, LANES), kept, (3 * count, LANES), (count, count)]
        + [(2 * count, LANES)] * 2,
        [parts, parts],
        *pieces,
    )
    states = (width, TILE, LANES)
    pair, other = both(pair, other)
    (base,) = call(functools.partial(mid_kernel, width), [states], [], keep, total)
    contact = functools.partial(step_kernel, width, patches, corners)
    outs = [states, tile, tile, tile, parts, parts]
    state, near, pair, other, *forces = call(
        contact, outs, [element_parts], keep, base, pair, other, indices, link, *spots, stiff
    )
    pair, other = both(pair, other)
    (total,) = call(
        functools.partial(spare_kernel, width, patches, corners),
        [tile],
        [(2 * element_parts[0], LANES)],
        keep, state, near, *spots, *forces, stiff,
    )
    outs = [(3, LANES), (3, LANES)]
    return tuple(call(end_kernel, outs, [], keep, state, total, pair, other, result=jax.ShapeDtypeStruct))


def solution(mesh):
    in_specs = (
        P(None, ("mx", "my")),
        P(None, ("mx", "my")),
        P(None, ("mx", "my")),
        P(("mx", "my")),
        P(None, ("mx", "my")),
        P(("mx", "my")),
        P(),
        P(None, ("mx", "my")),
        P(("mx", "my"), None),
        P(("mx", "my")),
        P(("mx", "my"), None),
    )
    out_specs = (P(None, ("mx", "my")), P(None, ("mx", "my")))
    return jax.shard_map(body, mesh=mesh, in_specs=in_specs, out_specs=out_specs, check_vma=False)
```

```python
import functools

import jax
import jax.numpy as jnp
from jax import lax
from jax.experimental import pallas as pl
from jax.experimental.pallas import tpu as pltpu
from jax.sharding import PartitionSpec as P


time_step = 0.1
penalty = 4.0
damping = 0.5
contact_reach = 4.0
LANES = 128
TILE = 8
FINE = 32
VMEM_GRANT = 16 << 20
ROW_MASS, ROW_SPEED, ROW_OWNER, ROW_ELASTIC, ROW_LISTS, ROW_PATCH = 3, 4, 7, 8, 12, 16


def pick(rows, indices):
    return jnp.take_along_axis(rows, indices, axis=1)


def parted(indices):
    coarse = jnp.floor(indices * (1.0 / FINE))
    return coarse, indices - FINE * coarse


def put_parts(parts_ref, values, base=0):
    for c, value in enumerate(values):
        high = value.astype(jnp.bfloat16).astype(jnp.float32)
        rest = value - high
        for b in range(value.shape[0] // TILE):
            at = base + b * TILE * TILE
            parts_ref[at + c * TILE : at + (c + 1) * TILE, :] = high[b * TILE : (b + 1) * TILE]
            parts_ref[at + (4 + c) * TILE : at + (5 + c) * TILE, :] = rest[b * TILE : (b + 1) * TILE]


def get_parts(parts_ref, row):
    if isinstance(row, int):
        start = row // TILE * TILE * TILE + row % TILE
    else:
        start = lax.div(row, TILE) * (TILE * TILE) + lax.rem(row, TILE)
    return parts_ref[pl.ds(start, TILE, stride=TILE), :]


def scatter(entries, chains=2):
    blocks = LANES // FINE
    tiles = []
    for first in range(min(chains, len(entries))):
        total = jnp.zeros((blocks * TILE, FINE), jnp.float32)
        for coarse, fine, weights in entries[first::chains]:
            wide = weights.shape[1]
            shape = (blocks * TILE, wide)
            block = (lax.broadcasted_iota(jnp.int32, shape, 0) // TILE).astype(jnp.float32).astype(jnp.bfloat16)
            placed = jnp.where(
                jnp.broadcast_to(coarse, shape).astype(jnp.bfloat16) == block,
                jnp.concatenate([weights] * blocks, axis=0).astype(jnp.bfloat16),
                jnp.zeros(shape, jnp.bfloat16),
            )
            shape = (FINE, wide)
            node = lax.broadcasted_iota(jnp.int32, shape, 0).astype(jnp.float32).astype(jnp.bfloat16)
            hot = jnp.where(
                jnp.broadcast_to(fine, shape).astype(jnp.bfloat16) == node,
                jnp.ones(shape, jnp.bfloat16),
                jnp.zeros(shape, jnp.bfloat16),
            )
            total += lax.dot_general(placed, hot, (((1,), (1,)), ((), ())), preferred_element_type=jnp.float32)
        tile = jnp.concatenate([total[b * TILE : (b + 1) * TILE] for b in range(blocks)], axis=1)
        tiles.append(tile + pltpu.roll(tile, 4, 0))
    return sum(tiles[1:], tiles[0])


def joined(entries):
    return [
        tuple(jnp.concatenate([a, b], axis=1) for a, b in zip(*two)) for two in zip(entries[0::2], entries[1::2])
    ]


def tile_parts(tile):
    high = tile.astype(jnp.bfloat16).astype(jnp.float32)
    rest = pltpu.roll(tile - high, 4, 0)
    row = lax.broadcasted_iota(jnp.int32, tile.shape, 0)
    return jnp.where(row < 4, high, rest)


def product(left, right):
    def parts(x):
        high = x.astype(jnp.bfloat16)
        return high, (x - high.astype(jnp.float32)).astype(jnp.bfloat16)

    (lh, lr), (rh, rr) = parts(left), parts(right)
    return sum(jnp.dot(a, b, preferred_element_type=jnp.float32) for a, b in ((lh, rh), (lr, rh), (lh, rr)))


def elastic_entries(units, stiffness, parts_ref):
    local, moduli = [], []
    for place, rest, connect, modulus in units:
        moved = place - rest
        for corners, scale in zip(connect, modulus):
            local.append(
                jnp.concatenate(
                    [
                        pick(jnp.broadcast_to(moved[c : c + 1], corners.shape), corners.astype(jnp.int32))
                        for c in range(3)
                    ],
                    axis=0,
                )
            )
            moduli.append(scale)
    forces = -jnp.concatenate(moduli, axis=1) * product(stiffness, jnp.concatenate(local, axis=1))
    lists, at = [], 0
    for _, _, connect, _ in units:
        base, count = at, connect[0].shape[0]
        for k in range(len(connect)):
            span = slice((at + k) * LANES, (at + k + 1) * LANES)
            put_parts(
                parts_ref, [forces[c * count : (c + 1) * count, span] for c in range(3)], (at + k) * count * TILE
            )
        split = [parted(corners) for corners in connect]
        lists.append(
            [
                (
                    jnp.concatenate([coarse[a : a + 1] for coarse, _ in split], axis=1),
                    jnp.concatenate([fine[a : a + 1] for _, fine in split], axis=1),
                    jnp.concatenate([get_parts(parts_ref, (base + k) * count + a) for k in range(len(connect))], axis=1),
                )
                for a in range(count)
            ]
        )
        at += len(connect)
    return lists


def pair_forces(mine, partner):
    offset = [b - a for a, b in zip(mine[:3], partner[:3])]
    distance = offset[0] * offset[0] + offset[1] * offset[1] + offset[2] * offset[2]
    weight = jnp.exp(-distance / contact_reach)
    return [
        -penalty * weight * o + damping * weight * (b - a)
        for o, a, b in zip(offset, mine[3:], partner[3:])
    ]


def choose(rows, device):
    chosen = jnp.broadcast_to(rows[0], device.shape)
    for d, row in enumerate(rows[1:], 1):
        chosen = jnp.where(device == d, row, chosen)
    return chosen


def pack_kernel(
    place_ref, speed_ref, rest_ref, mass_ref, connect_ref, modulus_ref, stiff_ref, lists_ref, patch_ref, owner_ref,
    map_ref, out_ref, mesh_ref, keep_ref, parts_ref,
):
    patches = patch_ref.shape[0]
    corners, elements = connect_ref.shape
    runs = [slice(k * LANES, (k + 1) * LANES) for k in range(elements // LANES)]
    connect = [connect_ref[:, run].astype(jnp.float32) for run in runs]
    modulus = [modulus_ref[:, run] for run in runs]
    (entries,) = elastic_entries([(place_ref[...], rest_ref[...], connect, modulus)], stiff_ref[...], parts_ref)
    keep_ref[...] = stiff_ref[...]
    out_ref[0:3, :] = place_ref[...]
    out_ref[ROW_MASS : ROW_MASS + 1, :] = mass_ref[...]
    out_ref[ROW_SPEED : ROW_SPEED + 3, :] = speed_ref[...]
    out_ref[ROW_OWNER : ROW_OWNER + 1, :] = jnp.zeros((1, LANES), jnp.float32)
    out_ref[ROW_OWNER : ROW_OWNER + 1, 0:patches] = owner_ref[...].astype(jnp.float32)
    out_ref[ROW_PATCH : ROW_PATCH + patches, :] = patch_ref[...].astype(jnp.float32)
    out_ref[ROW_PATCH + patches : ROW_PATCH + 2 * patches, :] = map_ref[...].astype(jnp.float32)
    for k in range(len(runs)):
        mesh_ref[k * corners : (k + 1) * corners, :] = connect[k]
    last = len(runs) * corners
    mesh_ref[last : last + TILE, :] = jnp.zeros((TILE, LANES), jnp.float32)
    mesh_ref[last : last + 3, :] = rest_ref[...]
    for k, scale in enumerate(modulus):
        mesh_ref[last + 4 + k : last + 5 + k, :] = scale
    out_ref[ROW_ELASTIC : ROW_ELASTIC + TILE, :] = scatter(entries)
    out_ref[ROW_LISTS : ROW_LISTS + 4, :] = lists_ref[...].astype(jnp.float32)


def route(table, rows):
    return jnp.dot(table, rows.astype(jnp.bfloat16), preferred_element_type=jnp.float32)


def put_contact(width, patches, state, indices, back, parts_ref, back_ref):
    count = width * patches
    nodes, target, device = [part.astype(jnp.int32) for part in indices]
    mine, partner = [], []
    for c in (0, 1, 2, 4, 5, 6):
        rows = [tile[c : c + 1] for tile in state]
        own = jnp.concatenate([jnp.broadcast_to(row, (patches, LANES)) for row in rows], axis=0)
        mine.append(pick(own, nodes))
        partner.append(pick(choose(rows, device), target))
    forces = pair_forces(mine, partner)
    put_parts(parts_ref, forces)
    for c, force in enumerate(forces):
        high = force.astype(jnp.bfloat16).astype(jnp.float32)
        for g, part in ((c, high), (4 + c, force - high)):
            routed = -route(back, part)
            for b in range(count // TILE):
                at = b * TILE * TILE + g * TILE
                back_ref[at : at + TILE, :] = routed[b * TILE : (b + 1) * TILE]


def contact_entries(width, patches, u, coarse_ref, fine_ref, parts_ref, back_ref):
    entries = []
    for base, ref in ((0, parts_ref), (width * patches, back_ref)):
        for s in range(patches):
            at = u * patches + s
            entries.append((coarse_ref[pl.ds(base + at, 1), :], fine_ref[pl.ds(base + at, 1), :], get_parts(ref, at)))
    return joined(entries)


def each_unit(width, unit):
    if width <= 4:
        for u in range(width):
            unit(u)
    else:
        lax.fori_loop(0, width, lambda u, carry: (unit(u), carry)[1], 0)


def face_values(tile, row):
    return pick(tile, jnp.broadcast_to(row.astype(jnp.int32), tile.shape))


def row_kernel(width, patches, where, *refs):
    total_ref, pair_ref, other_ref, keep_ref, idx_ref, link_ref, coarse_ref, fine_ref, parts_ref, back_ref = refs[-10:]
    me = lax.axis_index("my")
    side = lax.rem(lax.axis_index("mx"), 2)
    count = width * patches
    record = [refs[piece].at[place] for piece, place in where]
    state = [ref[0:TILE, :] for ref in record]
    nodes = jnp.concatenate([ref[ROW_PATCH : ROW_PATCH + patches, :] for ref in record], axis=0)
    pairs = jnp.concatenate([ref[ROW_PATCH + patches : ROW_PATCH + 2 * patches, :] for ref in record], axis=0)
    for s, ref in enumerate(record):
        keep_ref[s] = ref[0:ROW_PATCH, :]
    lane = lax.broadcasted_iota(jnp.int32, (patches, LANES), 1)
    line = lax.broadcasted_iota(jnp.int32, (patches, LANES), 0)
    owner_col = jnp.concatenate(
        [
            jnp.sum(jnp.where(lane == line, state[u][ROW_OWNER : ROW_OWNER + 1], 0.0), axis=1, keepdims=True)
            for u in range(width)
        ],
        axis=0,
    )
    row, col = [lax.broadcasted_iota(jnp.int32, (count, count), axis) for axis in (0, 1)]
    owner_row = jnp.sum(jnp.where(row == col, owner_col, 0.0), axis=0, keepdims=True)
    p, q = [(((at // patches) ^ me) * patches + at % patches).astype(jnp.float32) for at in (row, col)]
    same = owner_col == owner_row
    after = jnp.min(jnp.where(same, jnp.where(q > p, q, q + count), 3.0 * count), axis=1, keepdims=True)
    after = jnp.where(after >= count, after - count, after)
    before = jnp.max(jnp.where(same, jnp.where(q < p, q + count, q), -1.0), axis=1, keepdims=True)
    before = jnp.where(before >= count, before - count, before)
    link = jnp.where(q == after, 1.0, 0.0).astype(jnp.bfloat16)
    back = jnp.where(q == before, 1.0, 0.0)
    link_ref[...] = back
    back = back.astype(jnp.bfloat16)
    target = pick(route(link, nodes), pairs.astype(jnp.int32))
    device = jnp.broadcast_to(jnp.floor(after / patches).astype(jnp.int32) ^ me, (count, LANES)).astype(jnp.float32)
    idx_ref[0:count, :] = nodes
    idx_ref[count : 2 * count, :] = target
    idx_ref[2 * count : 3 * count, :] = device
    coarse, fine = parted(jnp.concatenate([nodes, route(back, target)], axis=0))
    coarse_ref[...] = coarse
    fine_ref[...] = fine
    put_contact(width, patches, state, (nodes, target, device), back, parts_ref, back_ref)

    def unit(u):
        info = keep_ref[u, ROW_ELASTIC : ROW_ELASTIC + TILE, :]
        total = scatter(contact_entries(width, patches, u, coarse_ref, fine_ref, parts_ref, back_ref), 1) + info
        total_ref[u] = total
        low, high = face_values(total, info[4:5]), face_values(total, info[5:6])
        pair_ref[u] = jnp.where(side == 0, high, low)[0:4]
        other_ref[u] = jnp.where(side == 0, low, high)[0:4]

    each_unit(width, unit)


def faces(tiles, lists):
    return scatter(joined([(*parted(row), tile_parts(tile)) for row, tile in zip(lists, tiles)]))


def inside(axis):
    at, size = lax.axis_index(axis), lax.axis_size(axis)
    partner = at - 1 + 2 * lax.rem(at, 2)
    return jnp.logical_and(partner >= 0, partner < size)


def mid_kernel(width, keep_ref, total_ref, base_ref):
    me = lax.axis_index("my")

    def unit(s):
        info = keep_ref[s, 0 : 2 * TILE, :]
        u = me ^ s
        down, up = jnp.maximum(u - 1, 0) ^ me, jnp.minimum(u + 1, width - 1) ^ me
        low = face_values(total_ref[down], keep_ref[down, ROW_LISTS + 3 : ROW_LISTS + 4, :])
        high = face_values(total_ref[up], keep_ref[up, ROW_LISTS + 2 : ROW_LISTS + 3, :])
        tiles = [jnp.where(u > 0, low, 0.0), jnp.where(u < width - 1, high, 0.0)]
        total = total_ref[s] + faces(tiles, [info[ROW_LISTS + 2 : ROW_LISTS + 3], info[ROW_LISTS + 3 : ROW_LISTS + 4]])
        mass = info[ROW_MASS : ROW_MASS + 1]
        base_ref[s, 0:4, :] = info[0:4]
        base_ref[s, 4:7, :] = info[ROW_SPEED : ROW_SPEED + 3] + time_step * mass * total[0:3]

    each_unit(width, unit)


def mx_faces(lists, pair, other):
    side = lax.rem(lax.axis_index("mx"), 2)
    near, far = jnp.where(side == 0, lists[1:2], lists[0:1]), jnp.where(side == 0, lists[0:1], lists[1:2])
    return faces([pair, jnp.where(inside("mx"), other, 0.0)], [near, far])


def elements_of(mesh, state, corners):
    last = mesh.shape[0] - TILE
    runs = last // corners
    connect = [mesh[k * corners : (k + 1) * corners] for k in range(runs)]
    return state[0:3], mesh[last : last + 3], connect, [mesh[last + 4 + k : last + 5 + k] for k in range(runs)]


def step_kernel(
    width, patches, corners, keep_ref, base_ref, pair_ref, other_ref, idx_ref, link_ref, coarse_ref, fine_ref, stiff_ref,
    mesh_ref, next_ref, near_ref, send_ref, far_ref, parts_ref, back_ref, element_ref,
):
    side = lax.rem(lax.axis_index("mx"), 2)
    count = width * patches
    blank = jnp.zeros((4, LANES), jnp.float32)

    def unit(s):
        base = base_ref[s]
        lists = keep_ref[s, ROW_LISTS : ROW_LISTS + 4, :]
        pair, other = [jnp.concatenate([ref[s], blank], axis=0) for ref in (pair_ref, other_ref)]
        speed = base[4:7] + time_step * base[3:4] * mx_faces(lists, pair, other)[0:3]
        next_ref[s, 0:3, :] = base[0:3] + time_step * speed
        next_ref[s, 4:7, :] = speed

    each_unit(width, unit)
    (elastic,) = elastic_entries([elements_of(mesh_ref[...], next_ref[0], corners)], stiff_ref[...], element_ref)
    state = [next_ref[s] for s in range(width)]
    indices = [idx_ref[g * count : (g + 1) * count, :] for g in range(3)]
    put_contact(width, patches, state, indices, link_ref[...].astype(jnp.bfloat16), parts_ref, back_ref)
    total = scatter(elastic + contact_entries(width, patches, 0, coarse_ref, fine_ref, parts_ref, back_ref))
    near_ref[...] = total
    lists = keep_ref[0, ROW_LISTS : ROW_LISTS + 4, :]
    low, high = face_values(total, lists[0:1]), face_values(total, lists[1:2])
    send_ref[...] = jnp.where(side == 0, high, low)
    far_ref[...] = jnp.where(side == 0, low, high)


def spare_kernel(
    width, patches, corners, keep_ref, next_ref, near_ref, coarse_ref, fine_ref, parts_ref, back_ref, stiff_ref,
    pair_ref, other_ref, total_ref, element_ref,
):
    me = lax.axis_index("my")
    around = [jnp.maximum(me - 1, 0) ^ me, jnp.minimum(me + 1, width - 1) ^ me]
    even = lax.rem(me, 2) == 0
    pair, other = pair_ref[...], other_ref[...]
    meshes = [jnp.where(even, other, pair), jnp.where(even, pair, other)]
    there = [me > 0, me < width - 1]
    units = [
        elements_of(jnp.where(exists, mesh, 0.0), next_ref[s], corners) for exists, mesh, s in zip(there, meshes, around)
    ]
    elastic = elastic_entries(units, stiff_ref[...], element_ref)
    below, above = [
        scatter(entries + contact_entries(width, patches, s, coarse_ref, fine_ref, parts_ref, back_ref), 1)
        for s, entries in zip(around, elastic)
    ]
    low = face_values(below, keep_ref[around[0], ROW_LISTS + 3 : ROW_LISTS + 4, :])
    high = face_values(above, keep_ref[around[1], ROW_LISTS + 2 : ROW_LISTS + 3, :])
    lists = keep_ref[0, ROW_LISTS : ROW_LISTS + 4, :]
    tiles = [jnp.where(exists, face, 0.0) for exists, face in zip(there, (low, high))]
    total_ref[...] = near_ref[...] + faces(tiles, [lists[2:3], lists[3:4]])


def end_kernel(keep_ref, next_ref, total_ref, pair_ref, other_ref, place_ref, speed_ref):
    lists = keep_ref[0, ROW_LISTS : ROW_LISTS + 4, :]
    total = total_ref[...] + mx_faces(lists, pair_ref[...], other_ref[...])
    speed = next_ref[0, 4:7, :] + time_step * keep_ref[0, ROW_MASS : ROW_MASS + 1, :] * total[0:3]
    speed_ref[...] = speed
    place_ref[...] = next_ref[0, 0:3, :] + time_step * speed


def call(kernel, outs, scratch, *args, result=pltpu.VMEM, placed=True):
    return pl.pallas_call(
        kernel,
        out_shape=[result(shape, jnp.float32) for shape in outs],
        in_specs=[pl.BlockSpec(memory_space=pltpu.VMEM)] * len(args),
        out_specs=[pl.BlockSpec(memory_space=pltpu.VMEM)] * len(outs),
        scratch_shapes=[pltpu.VMEM(shape, jnp.float32) for shape in scratch],
        compiler_params=pltpu.CompilerParams(vmem_limit_bytes=VMEM_GRANT if placed else None),
    )(*[pltpu.with_memory_space_constraint(arg, pltpu.VMEM) if placed else arg for arg in args])


def swap(value, axis, first, other):
    size, depth = lax.axis_size(axis), lax.axis_size(other)
    axes = ("mx", "my")
    place = (lambda i, k: i * depth + k) if axis == axes[0] else (lambda i, k: k * size + i)
    pairs = []
    for i in range(size):
        partner = i + 1 - 2 * ((i - first) % 2)
        for k in range(depth):
            if 0 <= partner < size:
                pairs.append((place(i, k), place(partner, k)))
            elif depth % 2 == 0:
                pairs.append((place(i, k), place(i, k ^ 1)))
    return lax.ppermute(value, axes, pairs)


def both(pair, other):
    other = swap(other, "mx", 1, "my")
    pair = swap(pair, "mx", 0, "my")
    return pair, other


def gather_row(record, axis):
    size = lax.axis_size(axis)
    steps = [size >> k for k in range(1, size.bit_length())]

    def exchange(value, step):
        return lax.ppermute(value, axis, [(i, i ^ step) for i in range(size)])

    direct = []
    for step in steps:
        direct.append(exchange(record[None], step))
    pieces, slots = [record[None]], [[0]]
    for step, near in zip(steps, direct):
        far, far_slots = pieces[1:], [s ^ step for held in slots[1:] for s in held]
        pieces, slots = pieces + [near], slots + [[step]]
        if far:
            pieces.append(exchange(far[0] if len(far) == 1 else jnp.concatenate(far, axis=0), step))
            slots.append(far_slots)
    where = {s: (n, k) for n, held in enumerate(slots) for k, s in enumerate(held)}
    return pieces, [where[s] for s in range(size)]


def body(
    positions, velocities, rest_positions, inverse_mass, element_nodes, modulus, stiffness, shared_lists, patch_nodes,
    patch_owner, pair_map,
):
    width = lax.axis_size("my")
    patches = patch_owner.shape[0]
    corners, elements = element_nodes.shape
    count = width * patches
    modulus, mass = modulus[None], inverse_mass[None]
    runs = elements // LANES
    element_parts = (TILE * corners * runs, LANES)
    tile = (TILE, LANES)
    parts = (TILE * count, LANES)
    record, mesh, stiff = call(
        pack_kernel,
        [(ROW_PATCH + 2 * patches, LANES), (runs * corners + TILE, LANES), stiffness.shape],
        [element_parts],
        positions, velocities, rest_positions, mass, element_nodes, modulus, stiffness, shared_lists, patch_nodes,
        patch_owner[None], pair_map, placed=False,
    )
    pieces, where = gather_row(record, "my")
    kept = (width, ROW_PATCH, LANES)
    mesh_pair = swap(mesh, "my", 0, "mx")
    mesh_other = swap(mesh, "my", 1, "mx")
    total, pair, other, keep, indices, link, *spots = call(
        functools.partial(row_kernel, width, patches, where),
        [(width, TILE, LANES), (width, 4, LANES), (width, 4, LANES), kept, (3 * count, LANES), (count, count)]
        + [(2 * count, LANES)] * 2,
        [parts, parts],
        *pieces,
    )
    states = (width, TILE, LANES)
    pair, other = both(pair, other)
    (base,) = call(functools.partial(mid_kernel, width), [states], [], keep, total)
    contact = functools.partial(step_kernel, width, patches, corners)
    outs = [states, tile, tile, tile, parts, parts]
    state, near, pair, other, *forces = call(
        contact, outs, [element_parts], keep, base, pair, other, indices, link, *spots, stiff, mesh
    )
    pair, other = both(pair, other)
    (total,) = call(
        functools.partial(spare_kernel, width, patches, corners),
        [tile],
        [(2 * element_parts[0], LANES)],
        keep, state, near, *spots, *forces, stiff, mesh_pair, mesh_other,
    )
    outs = [(3, LANES), (3, LANES)]
    return tuple(call(end_kernel, outs, [], keep, state, total, pair, other, result=jax.ShapeDtypeStruct))


def solution(mesh):
    in_specs = (
        P(None, ("mx", "my")),
        P(None, ("mx", "my")),
        P(None, ("mx", "my")),
        P(("mx", "my")),
        P(None, ("mx", "my")),
        P(("mx", "my")),
        P(),
        P(None, ("mx", "my")),
        P(("mx", "my"), None),
        P(("mx", "my")),
        P(("mx", "my"), None),
    )
    out_specs = (P(None, ("mx", "my")), P(None, ("mx", "my")))
    return jax.shard_map(body, mesh=mesh, in_specs=in_specs, out_specs=out_specs, check_vma=False)
```

```python
import functools

import jax
import jax.numpy as jnp
from jax import lax
from jax.experimental import pallas as pl
from jax.experimental.pallas import tpu as pltpu
from jax.sharding import PartitionSpec as P


time_step = 0.1
penalty = 4.0
damping = 0.5
contact_reach = 4.0
LANES = 128
TILE = 8
FINE = 32
VMEM_GRANT = 16 << 20
ROW_MASS, ROW_SPEED, ROW_OWNER, ROW_ELASTIC, ROW_LISTS, ROW_PATCH = 3, 4, 7, 8, 12, 16


def pick(rows, indices):
    return jnp.take_along_axis(rows, indices, axis=1)


def parted(indices):
    coarse = jnp.floor(indices * (1.0 / FINE))
    return coarse, indices - FINE * coarse


def put_parts(parts_ref, values, base=0):
    for c, value in enumerate(values):
        high = value.astype(jnp.bfloat16).astype(jnp.float32)
        rest = value - high
        for b in range(value.shape[0] // TILE):
            at = base + b * TILE * TILE
            parts_ref[at + c * TILE : at + (c + 1) * TILE, :] = high[b * TILE : (b + 1) * TILE]
            parts_ref[at + (4 + c) * TILE : at + (5 + c) * TILE, :] = rest[b * TILE : (b + 1) * TILE]


def get_parts(parts_ref, row):
    if isinstance(row, int):
        start = row // TILE * TILE * TILE + row % TILE
    else:
        start = lax.div(row, TILE) * (TILE * TILE) + lax.rem(row, TILE)
    return parts_ref[pl.ds(start, TILE, stride=TILE), :]


def scatter(entries, chains=2):
    blocks = LANES // FINE
    tiles = []
    for first in range(min(chains, len(entries))):
        total = jnp.zeros((blocks * TILE, FINE), jnp.float32)
        for coarse, fine, weights in entries[first::chains]:
            wide = weights.shape[1]
            shape = (blocks * TILE, wide)
            block = (lax.broadcasted_iota(jnp.int32, shape, 0) // TILE).astype(jnp.float32).astype(jnp.bfloat16)
            placed = jnp.where(
                jnp.broadcast_to(coarse, shape).astype(jnp.bfloat16) == block,
                jnp.concatenate([weights] * blocks, axis=0).astype(jnp.bfloat16),
                jnp.zeros(shape, jnp.bfloat16),
            )
            shape = (FINE, wide)
            node = lax.broadcasted_iota(jnp.int32, shape, 0).astype(jnp.float32).astype(jnp.bfloat16)
            hot = jnp.where(
                jnp.broadcast_to(fine, shape).astype(jnp.bfloat16) == node,
                jnp.ones(shape, jnp.bfloat16),
                jnp.zeros(shape, jnp.bfloat16),
            )
            total += lax.dot_general(placed, hot, (((1,), (1,)), ((), ())), preferred_element_type=jnp.float32)
        tile = jnp.concatenate([total[b * TILE : (b + 1) * TILE] for b in range(blocks)], axis=1)
        tiles.append(tile + pltpu.roll(tile, 4, 0))
    return sum(tiles[1:], tiles[0])


def joined(entries):
    return [
        tuple(jnp.concatenate([a, b], axis=1) for a, b in zip(*two)) for two in zip(entries[0::2], entries[1::2])
    ]


def tile_parts(tile):
    high = tile.astype(jnp.bfloat16).astype(jnp.float32)
    rest = pltpu.roll(tile - high, 4, 0)
    row = lax.broadcasted_iota(jnp.int32, tile.shape, 0)
    return jnp.where(row < 4, high, rest)


def product(left, right):
    def parts(x):
        high = x.astype(jnp.bfloat16)
        return high, (x - high.astype(jnp.float32)).astype(jnp.bfloat16)

    (lh, lr), (rh, rr) = parts(left), parts(right)
    return sum(jnp.dot(a, b, preferred_element_type=jnp.float32) for a, b in ((lh, rh), (lr, rh), (lh, rr)))


def elastic_entries(units, stiffness, parts_ref):
    local, moduli = [], []
    for place, rest, connect, modulus in units:
        moved = place - rest
        for corners, scale in zip(connect, modulus):
            local.append(
                jnp.concatenate(
                    [
                        pick(jnp.broadcast_to(moved[c : c + 1], corners.shape), corners.astype(jnp.int32))
                        for c in range(3)
                    ],
                    axis=0,
                )
            )
            moduli.append(scale)
    forces = -jnp.concatenate(moduli, axis=1) * product(stiffness, jnp.concatenate(local, axis=1))
    lists, at = [], 0
    for _, _, connect, _ in units:
        base, count = at, connect[0].shape[0]
        for k in range(len(connect)):
            span = slice((at + k) * LANES, (at + k + 1) * LANES)
            put_parts(
                parts_ref, [forces[c * count : (c + 1) * count, span] for c in range(3)], (at + k) * count * TILE
            )
        split = [parted(corners) for corners in connect]
        lists.append(
            [
                (
                    jnp.concatenate([coarse[a : a + 1] for coarse, _ in split], axis=1),
                    jnp.concatenate([fine[a : a + 1] for _, fine in split], axis=1),
                    jnp.concatenate([get_parts(parts_ref, (base + k) * count + a) for k in range(len(connect))], axis=1),
                )
                for a in range(count)
            ]
        )
        at += len(connect)
    return lists


def pair_forces(mine, partner):
    offset = [b - a for a, b in zip(mine[:3], partner[:3])]
    distance = offset[0] * offset[0] + offset[1] * offset[1] + offset[2] * offset[2]
    weight = jnp.exp(-distance / contact_reach)
    return [
        -penalty * weight * o + damping * weight * (b - a)
        for o, a, b in zip(offset, mine[3:], partner[3:])
    ]


def choose(rows, device):
    chosen = jnp.broadcast_to(rows[0], device.shape)
    for d, row in enumerate(rows[1:], 1):
        chosen = jnp.where(device == d, row, chosen)
    return chosen


def pack_kernel(
    place_ref, speed_ref, rest_ref, mass_ref, connect_ref, modulus_ref, stiff_ref, lists_ref, patch_ref, owner_ref,
    map_ref, out_ref, mesh_ref, keep_ref, parts_ref,
):
    patches = patch_ref.shape[0]
    corners, elements = connect_ref.shape
    runs = [slice(k * LANES, (k + 1) * LANES) for k in range(elements // LANES)]
    connect = [connect_ref[:, run].astype(jnp.float32) for run in runs]
    modulus = [modulus_ref[:, run] for run in runs]
    (entries,) = elastic_entries([(place_ref[...], rest_ref[...], connect, modulus)], stiff_ref[...], parts_ref)
    keep_ref[...] = stiff_ref[...]
    out_ref[0:3, :] = place_ref[...]
    out_ref[ROW_MASS : ROW_MASS + 1, :] = mass_ref[...]
    out_ref[ROW_SPEED : ROW_SPEED + 3, :] = speed_ref[...]
    out_ref[ROW_OWNER : ROW_OWNER + 1, :] = jnp.zeros((1, LANES), jnp.float32)
    out_ref[ROW_OWNER : ROW_OWNER + 1, 0:patches] = owner_ref[...].astype(jnp.float32)
    out_ref[ROW_PATCH : ROW_PATCH + patches, :] = patch_ref[...].astype(jnp.float32)
    out_ref[ROW_PATCH + patches : ROW_PATCH + 2 * patches, :] = map_ref[...].astype(jnp.float32)
    for k in range(len(runs)):
        mesh_ref[k * corners : (k + 1) * corners, :] = connect[k]
    last = len(runs) * corners
    mesh_ref[last : last + TILE, :] = jnp.zeros((TILE, LANES), jnp.float32)
    mesh_ref[last : last + 3, :] = rest_ref[...]
    for k, scale in enumerate(modulus):
        mesh_ref[last + 4 + k : last + 5 + k, :] = scale
    out_ref[ROW_ELASTIC : ROW_ELASTIC + TILE, :] = scatter(entries)
    out_ref[ROW_LISTS : ROW_LISTS + 4, :] = lists_ref[...].astype(jnp.float32)


def route(table, rows):
    return jnp.dot(table, rows.astype(jnp.bfloat16), preferred_element_type=jnp.float32)


def put_contact(width, patches, state, indices, back, parts_ref, back_ref):
    count = width * patches
    nodes, target, device = [part.astype(jnp.int32) for part in indices]
    mine, partner = [], []
    for c in (0, 1, 2, 4, 5, 6):
        rows = [tile[c : c + 1] for tile in state]
        own = jnp.concatenate([jnp.broadcast_to(row, (patches, LANES)) for row in rows], axis=0)
        mine.append(pick(own, nodes))
        partner.append(pick(choose(rows, device), target))
    forces = pair_forces(mine, partner)
    put_parts(parts_ref, forces)
    for c, force in enumerate(forces):
        high = force.astype(jnp.bfloat16).astype(jnp.float32)
        for g, part in ((c, high), (4 + c, force - high)):
            routed = -route(back, part)
            for b in range(count // TILE):
                at = b * TILE * TILE + g * TILE
                back_ref[at : at + TILE, :] = routed[b * TILE : (b + 1) * TILE]


def contact_entries(patches, u, base, coarse_ref, fine_ref, parts_ref):
    entries = []
    for s in range(patches):
        at = u * patches + s
        entries.append((coarse_ref[pl.ds(base + at, 1), :], fine_ref[pl.ds(base + at, 1), :], get_parts(parts_ref, at)))
    return joined(entries)


def each_unit(width, unit):
    if width <= 4:
        for u in range(width):
            unit(u)
    else:
        lax.fori_loop(0, width, lambda u, carry: (unit(u), carry)[1], 0)


def face_values(tile, row):
    return pick(tile, jnp.broadcast_to(row.astype(jnp.int32), tile.shape))


def row_kernel(width, patches, where, *refs):
    total_ref, pair_ref, other_ref, keep_ref, idx_ref, link_ref, coarse_ref, fine_ref, parts_ref, back_ref = refs[-10:]
    me = lax.axis_index("my")
    side = lax.rem(lax.axis_index("mx"), 2)
    count = width * patches
    record = [refs[piece].at[place] for piece, place in where]
    state = [ref[0:TILE, :] for ref in record]
    nodes = jnp.concatenate([ref[ROW_PATCH : ROW_PATCH + patches, :] for ref in record], axis=0)
    pairs = jnp.concatenate([ref[ROW_PATCH + patches : ROW_PATCH + 2 * patches, :] for ref in record], axis=0)
    for s, ref in enumerate(record):
        keep_ref[s] = ref[0:ROW_PATCH, :]
    lane = lax.broadcasted_iota(jnp.int32, (patches, LANES), 1)
    line = lax.broadcasted_iota(jnp.int32, (patches, LANES), 0)
    owner_col = jnp.concatenate(
        [
            jnp.sum(jnp.where(lane == line, state[u][ROW_OWNER : ROW_OWNER + 1], 0.0), axis=1, keepdims=True)
            for u in range(width)
        ],
        axis=0,
    )
    row, col = [lax.broadcasted_iota(jnp.int32, (count, count), axis) for axis in (0, 1)]
    owner_row = jnp.sum(jnp.where(row == col, owner_col, 0.0), axis=0, keepdims=True)
    p, q = [(((at // patches) ^ me) * patches + at % patches).astype(jnp.float32) for at in (row, col)]
    same = owner_col == owner_row
    after = jnp.min(jnp.where(same, jnp.where(q > p, q, q + count), 3.0 * count), axis=1, keepdims=True)
    after = jnp.where(after >= count, after - count, after)
    before = jnp.max(jnp.where(same, jnp.where(q < p, q + count, q), -1.0), axis=1, keepdims=True)
    before = jnp.where(before >= count, before - count, before)
    link = jnp.where(q == after, 1.0, 0.0).astype(jnp.bfloat16)
    back = jnp.where(q == before, 1.0, 0.0)
    link_ref[...] = back
    back = back.astype(jnp.bfloat16)
    target = pick(route(link, nodes), pairs.astype(jnp.int32))
    device = jnp.broadcast_to(jnp.floor(after / patches).astype(jnp.int32) ^ me, (count, LANES)).astype(jnp.float32)
    idx_ref[0:count, :] = nodes
    idx_ref[count : 2 * count, :] = target
    idx_ref[2 * count : 3 * count, :] = device
    coarse, fine = parted(jnp.concatenate([nodes, route(back, target)], axis=0))
    coarse_ref[...] = coarse
    fine_ref[...] = fine
    put_contact(width, patches, state, (nodes, target, device), back, parts_ref, back_ref)

    def direct(u):
        info = keep_ref[u, ROW_ELASTIC : ROW_ELASTIC + TILE, :]
        total_ref[u] = scatter(contact_entries(patches, u, 0, coarse_ref, fine_ref, parts_ref), 1) + info

    def unit(u):
        info = keep_ref[u, ROW_ELASTIC : ROW_ELASTIC + TILE, :]
        total = total_ref[u] + scatter(contact_entries(patches, u, count, coarse_ref, fine_ref, back_ref), 1)
        total_ref[u] = total
        low, high = face_values(total, info[4:5]), face_values(total, info[5:6])
        pair_ref[u] = jnp.where(side == 0, high, low)[0:4]
        other_ref[u] = jnp.where(side == 0, low, high)[0:4]

    each_unit(width, direct)
    each_unit(width, unit)


def faces(tiles, lists):
    return scatter(joined([(*parted(row), tile_parts(tile)) for row, tile in zip(lists, tiles)]))


def inside(axis):
    at, size = lax.axis_index(axis), lax.axis_size(axis)
    partner = at - 1 + 2 * lax.rem(at, 2)
    return jnp.logical_and(partner >= 0, partner < size)


def mid_kernel(width, patches, keep_ref, total_ref, idx_ref, link_ref, base_ref, table_ref):
    me = lax.axis_index("my")
    count = width * patches
    back = link_ref[0:patches, :].astype(jnp.bfloat16)
    nodes, target, device = [idx_ref[g * count : (g + 1) * count, :] for g in range(3)]
    slot = (lax.broadcasted_iota(jnp.int32, (count, LANES), 0) // patches).astype(jnp.float32)
    table = [
        nodes[0:patches],
        route(back, target),
        target[0:patches],
        route(back, nodes),
        device[0:patches],
        route(back, slot),
    ]
    for g, rows in enumerate(table):
        table_ref[g * patches : (g + 1) * patches, :] = rows

    def unit(s):
        info = keep_ref[s, 0 : 2 * TILE, :]
        u = me ^ s
        down, up = jnp.maximum(u - 1, 0) ^ me, jnp.minimum(u + 1, width - 1) ^ me
        low = face_values(total_ref[down], keep_ref[down, ROW_LISTS + 3 : ROW_LISTS + 4, :])
        high = face_values(total_ref[up], keep_ref[up, ROW_LISTS + 2 : ROW_LISTS + 3, :])
        tiles = [jnp.where(u > 0, low, 0.0), jnp.where(u < width - 1, high, 0.0)]
        total = total_ref[s] + faces(tiles, [info[ROW_LISTS + 2 : ROW_LISTS + 3], info[ROW_LISTS + 3 : ROW_LISTS + 4]])
        mass = info[ROW_MASS : ROW_MASS + 1]
        base_ref[s, 0:4, :] = info[0:4]
        base_ref[s, 4:7, :] = info[ROW_SPEED : ROW_SPEED + 3] + time_step * mass * total[0:3]

    each_unit(width, unit)


def mx_faces(lists, pair, other):
    side = lax.rem(lax.axis_index("mx"), 2)
    near, far = jnp.where(side == 0, lists[1:2], lists[0:1]), jnp.where(side == 0, lists[0:1], lists[1:2])
    return faces([pair, jnp.where(inside("mx"), other, 0.0)], [near, far])


def elements_of(mesh, state, corners):
    last = mesh.shape[0] - TILE
    runs = last // corners
    connect = [mesh[k * corners : (k + 1) * corners] for k in range(runs)]
    return state[0:3], mesh[last : last + 3], connect, [mesh[last + 4 + k : last + 5 + k] for k in range(runs)]


def step_kernel(
    width, patches, corners, keep_ref, base_ref, pair_ref, other_ref, table_ref, stiff_ref, mesh_ref,
    next_ref, near_ref, send_ref, far_ref, parts_ref, element_ref,
):
    side = lax.rem(lax.axis_index("mx"), 2)
    blank = jnp.zeros((4, LANES), jnp.float32)

    def unit(s):
        base = base_ref[s]
        lists = keep_ref[s, ROW_LISTS : ROW_LISTS + 4, :]
        pair, other = [jnp.concatenate([ref[s], blank], axis=0) for ref in (pair_ref, other_ref)]
        speed = base[4:7] + time_step * base[3:4] * mx_faces(lists, pair, other)[0:3]
        next_ref[s, 0:3, :] = base[0:3] + time_step * speed
        next_ref[s, 4:7, :] = speed

    each_unit(width, unit)
    (elastic,) = elastic_entries([elements_of(mesh_ref[...], next_ref[0], corners)], stiff_ref[...], element_ref)
    table = [table_ref[g * patches : (g + 1) * patches, :] for g in range(6)]
    nodes, landing, target, from_nodes, to_slot, from_slot = [rows.astype(jnp.int32) for rows in table]
    first, second = [], []
    for c in (0, 1, 2, 4, 5, 6):
        rows = [next_ref[s, c : c + 1, :] for s in range(width)]
        home = jnp.broadcast_to(rows[0], (patches, LANES))
        first.append(jnp.concatenate([pick(home, nodes), pick(choose(rows, from_slot), from_nodes)], axis=0))
        second.append(jnp.concatenate([pick(choose(rows, to_slot), target), pick(home, landing)], axis=0))
    sign = jnp.where(lax.broadcasted_iota(jnp.int32, (2 * patches, LANES), 0) < patches, 1.0, -1.0)
    put_parts(parts_ref, [sign * force for force in pair_forces(first, second)])
    coarse, fine = parted(table_ref[0 : 2 * patches, :])
    contact = [(coarse[k : k + 1], fine[k : k + 1], get_parts(parts_ref, k)) for k in range(2 * patches)]
    total = scatter(elastic + joined(contact))
    near_ref[...] = total
    lists = keep_ref[0, ROW_LISTS : ROW_LISTS + 4, :]
    low, high = face_values(total, lists[0:1]), face_values(total, lists[1:2])
    send_ref[...] = jnp.where(side == 0, high, low)
    far_ref[...] = jnp.where(side == 0, low, high)


def spare_kernel(
    width, patches, corners, keep_ref, next_ref, near_ref, idx_ref, link_ref, coarse_ref, fine_ref, stiff_ref,
    pair_ref, other_ref, total_ref, parts_ref, back_ref, element_ref,
):
    me = lax.axis_index("my")
    count = width * patches
    state = [next_ref[s] for s in range(width)]
    indices = [idx_ref[g * count : (g + 1) * count, :] for g in range(3)]
    put_contact(width, patches, state, indices, link_ref[...].astype(jnp.bfloat16), parts_ref, back_ref)
    around = [jnp.maximum(me - 1, 0) ^ me, jnp.minimum(me + 1, width - 1) ^ me]
    even = lax.rem(me, 2) == 0
    pair, other = pair_ref[...], other_ref[...]
    meshes = [jnp.where(even, other, pair), jnp.where(even, pair, other)]
    there = [me > 0, me < width - 1]
    units = [
        elements_of(jnp.where(exists, mesh, 0.0), next_ref[s], corners) for exists, mesh, s in zip(there, meshes, around)
    ]
    elastic = elastic_entries(units, stiff_ref[...], element_ref)
    below, above = [
        scatter(
            entries
            + contact_entries(patches, s, 0, coarse_ref, fine_ref, parts_ref)
            + contact_entries(patches, s, count, coarse_ref, fine_ref, back_ref),
            1,
        )
        for s, entries in zip(around, elastic)
    ]
    low = face_values(below, keep_ref[around[0], ROW_LISTS + 3 : ROW_LISTS + 4, :])
    high = face_values(above, keep_ref[around[1], ROW_LISTS + 2 : ROW_LISTS + 3, :])
    lists = keep_ref[0, ROW_LISTS : ROW_LISTS + 4, :]
    tiles = [jnp.where(exists, face, 0.0) for exists, face in zip(there, (low, high))]
    total_ref[...] = near_ref[...] + faces(tiles, [lists[2:3], lists[3:4]])


def end_kernel(keep_ref, next_ref, total_ref, pair_ref, other_ref, place_ref, speed_ref):
    lists = keep_ref[0, ROW_LISTS : ROW_LISTS + 4, :]
    total = total_ref[...] + mx_faces(lists, pair_ref[...], other_ref[...])
    speed = next_ref[0, 4:7, :] + time_step * keep_ref[0, ROW_MASS : ROW_MASS + 1, :] * total[0:3]
    speed_ref[...] = speed
    place_ref[...] = next_ref[0, 0:3, :] + time_step * speed


def call(kernel, outs, scratch, *args, result=pltpu.VMEM, placed=True):
    return pl.pallas_call(
        kernel,
        out_shape=[result(shape, jnp.float32) for shape in outs],
        in_specs=[pl.BlockSpec(memory_space=pltpu.VMEM)] * len(args),
        out_specs=[pl.BlockSpec(memory_space=pltpu.VMEM)] * len(outs),
        scratch_shapes=[pltpu.VMEM(shape, jnp.float32) for shape in scratch],
        compiler_params=pltpu.CompilerParams(vmem_limit_bytes=VMEM_GRANT if placed else None),
    )(*[pltpu.with_memory_space_constraint(arg, pltpu.VMEM) if placed else arg for arg in args])


def swap(value, axis, first, other):
    size, depth = lax.axis_size(axis), lax.axis_size(other)
    axes = ("mx", "my")
    place = (lambda i, k: i * depth + k) if axis == axes[0] else (lambda i, k: k * size + i)
    pairs = []
    for i in range(size):
        partner = i + 1 - 2 * ((i - first) % 2)
        for k in range(depth):
            if 0 <= partner < size:
                pairs.append((place(i, k), place(partner, k)))
            elif depth % 2 == 0:
                pairs.append((place(i, k), place(i, k ^ 1)))
    return lax.ppermute(value, axes, pairs)


def both(pair, other):
    other = swap(other, "mx", 1, "my")
    pair = swap(pair, "mx", 0, "my")
    return pair, other


def gather_row(record, axis):
    size = lax.axis_size(axis)
    steps = [size >> k for k in range(1, size.bit_length())]

    def exchange(value, step):
        return lax.ppermute(value, axis, [(i, i ^ step) for i in range(size)])

    direct = []
    for step in steps:
        direct.append(exchange(record[None], step))
    pieces, slots = [record[None]], [[0]]
    for step, near in zip(steps, direct):
        far, far_slots = pieces[1:], [s ^ step for held in slots[1:] for s in held]
        pieces, slots = pieces + [near], slots + [[step]]
        if far:
            pieces.append(exchange(far[0] if len(far) == 1 else jnp.concatenate(far, axis=0), step))
            slots.append(far_slots)
    where = {s: (n, k) for n, held in enumerate(slots) for k, s in enumerate(held)}
    return pieces, [where[s] for s in range(size)]


def body(
    positions, velocities, rest_positions, inverse_mass, element_nodes, modulus, stiffness, shared_lists, patch_nodes,
    patch_owner, pair_map,
):
    width = lax.axis_size("my")
    patches = patch_owner.shape[0]
    corners, elements = element_nodes.shape
    count = width * patches
    modulus, mass = modulus[None], inverse_mass[None]
    runs = elements // LANES
    element_parts = (TILE * corners * runs, LANES)
    tile = (TILE, LANES)
    parts = (TILE * count, LANES)
    record, mesh, stiff = call(
        pack_kernel,
        [(ROW_PATCH + 2 * patches, LANES), (runs * corners + TILE, LANES), stiffness.shape],
        [element_parts],
        positions, velocities, rest_positions, mass, element_nodes, modulus, stiffness, shared_lists, patch_nodes,
        patch_owner[None], pair_map, placed=False,
    )
    pieces, where = gather_row(record, "my")
    kept = (width, ROW_PATCH, LANES)
    mesh_pair = swap(mesh, "my", 0, "mx")
    mesh_other = swap(mesh, "my", 1, "mx")
    total, pair, other, keep, indices, link, *spots = call(
        functools.partial(row_kernel, width, patches, where),
        [(width, TILE, LANES), (width, 4, LANES), (width, 4, LANES), kept, (3 * count, LANES), (count, count)]
        + [(2 * count, LANES)] * 2,
        [parts, parts],
        *pieces,
    )
    states = (width, TILE, LANES)
    pair, other = both(pair, other)
    base, table = call(
        functools.partial(mid_kernel, width, patches),
        [states, (6 * patches, LANES)],
        [],
        keep, total, indices, link,
    )
    contact = functools.partial(step_kernel, width, patches, corners)
    state, near, pair, other = call(
        contact,
        [states, tile, tile, tile],
        [(TILE * 2 * patches, LANES), element_parts],
        keep, base, pair, other, table, stiff, mesh,
    )
    pair, other = both(pair, other)
    (total,) = call(
        functools.partial(spare_kernel, width, patches, corners),
        [tile],
        [parts, parts, (2 * element_parts[0], LANES)],
        keep, state, near, indices, link, *spots, stiff, mesh_pair, mesh_other,
    )
    outs = [(3, LANES), (3, LANES)]
    return tuple(call(end_kernel, outs, [], keep, state, total, pair, other, result=jax.ShapeDtypeStruct))


def solution(mesh):
    in_specs = (
        P(None, ("mx", "my")),
        P(None, ("mx", "my")),
        P(None, ("mx", "my")),
        P(("mx", "my")),
        P(None, ("mx", "my")),
        P(("mx", "my")),
        P(),
        P(None, ("mx", "my")),
        P(("mx", "my"), None),
        P(("mx", "my")),
        P(("mx", "my"), None),
    )
    out_specs = (P(None, ("mx", "my")), P(None, ("mx", "my")))
    return jax.shard_map(body, mesh=mesh, in_specs=in_specs, out_specs=out_specs, check_vma=False)
```

```python
import functools

import jax
import jax.numpy as jnp
from jax import lax
from jax.experimental import pallas as pl
from jax.experimental.pallas import tpu as pltpu
from jax.sharding import PartitionSpec as P


time_step = 0.1
penalty = 4.0
damping = 0.5
contact_reach = 4.0
LANES = 128
TILE = 8
FINE = 32
VMEM_GRANT = 16 << 20
ROW_MASS, ROW_SPEED, ROW_OWNER, ROW_ELASTIC, ROW_LISTS, ROW_PATCH = 3, 4, 7, 8, 12, 16


def pick(rows, indices):
    return jnp.take_along_axis(rows, indices, axis=1)


def parted(indices):
    coarse = jnp.floor(indices * (1.0 / FINE))
    return coarse, indices - FINE * coarse


def put_parts(parts_ref, values, base=0):
    for c, value in enumerate(values):
        high = value.astype(jnp.bfloat16).astype(jnp.float32)
        rest = value - high
        for b in range(value.shape[0] // TILE):
            at = base + b * TILE * TILE
            parts_ref[at + c * TILE : at + (c + 1) * TILE, :] = high[b * TILE : (b + 1) * TILE]
            parts_ref[at + (4 + c) * TILE : at + (5 + c) * TILE, :] = rest[b * TILE : (b + 1) * TILE]


def get_parts(parts_ref, row):
    if isinstance(row, int):
        start = row // TILE * TILE * TILE + row % TILE
    else:
        start = lax.div(row, TILE) * (TILE * TILE) + lax.rem(row, TILE)
    return parts_ref[pl.ds(start, TILE, stride=TILE), :]


def scatter(entries, chains=2):
    blocks = LANES // FINE
    tiles = []
    for first in range(min(chains, len(entries))):
        total = jnp.zeros((blocks * TILE, FINE), jnp.float32)
        for coarse, fine, weights in entries[first::chains]:
            wide = weights.shape[1]
            shape = (blocks * TILE, wide)
            block = (lax.broadcasted_iota(jnp.int32, shape, 0) // TILE).astype(jnp.float32).astype(jnp.bfloat16)
            placed = jnp.where(
                jnp.broadcast_to(coarse, shape).astype(jnp.bfloat16) == block,
                jnp.concatenate([weights] * blocks, axis=0).astype(jnp.bfloat16),
                jnp.zeros(shape, jnp.bfloat16),
            )
            shape = (FINE, wide)
            node = lax.broadcasted_iota(jnp.int32, shape, 0).astype(jnp.float32).astype(jnp.bfloat16)
            hot = jnp.where(
                jnp.broadcast_to(fine, shape).astype(jnp.bfloat16) == node,
                jnp.ones(shape, jnp.bfloat16),
                jnp.zeros(shape, jnp.bfloat16),
            )
            total += lax.dot_general(placed, hot, (((1,), (1,)), ((), ())), preferred_element_type=jnp.float32)
        tile = jnp.concatenate([total[b * TILE : (b + 1) * TILE] for b in range(blocks)], axis=1)
        tiles.append(tile + pltpu.roll(tile, 4, 0))
    return sum(tiles[1:], tiles[0])


def joined(entries):
    return [
        tuple(jnp.concatenate([a, b], axis=1) for a, b in zip(*two)) for two in zip(entries[0::2], entries[1::2])
    ]


def tile_parts(tile):
    high = tile.astype(jnp.bfloat16).astype(jnp.float32)
    rest = pltpu.roll(tile - high, 4, 0)
    row = lax.broadcasted_iota(jnp.int32, tile.shape, 0)
    return jnp.where(row < 4, high, rest)


def product(left, right):
    def parts(x):
        high = x.astype(jnp.bfloat16)
        return high, (x - high.astype(jnp.float32)).astype(jnp.bfloat16)

    (lh, lr), (rh, rr) = parts(left), parts(right)
    return sum(jnp.dot(a, b, preferred_element_type=jnp.float32) for a, b in ((lh, rh), (lr, rh), (lh, rr)))


def elastic_entries(units, stiffness, parts_ref):
    local, moduli = [], []
    for place, rest, connect, modulus in units:
        moved = place - rest
        for corners, scale in zip(connect, modulus):
            local.append(
                jnp.concatenate(
                    [
                        pick(jnp.broadcast_to(moved[c : c + 1], corners.shape), corners.astype(jnp.int32))
                        for c in range(3)
                    ],
                    axis=0,
                )
            )
            moduli.append(scale)
    forces = -jnp.concatenate(moduli, axis=1) * product(stiffness, jnp.concatenate(local, axis=1))
    lists, at = [], 0
    for _, _, connect, _ in units:
        base, count = at, connect[0].shape[0]
        for k in range(len(connect)):
            span = slice((at + k) * LANES, (at + k + 1) * LANES)
            put_parts(
                parts_ref, [forces[c * count : (c + 1) * count, span] for c in range(3)], (at + k) * count * TILE
            )
        split = [parted(corners) for corners in connect]
        lists.append(
            [
                (
                    jnp.concatenate([coarse[a : a + 1] for coarse, _ in split], axis=1),
                    jnp.concatenate([fine[a : a + 1] for _, fine in split], axis=1),
                    jnp.concatenate([get_parts(parts_ref, (base + k) * count + a) for k in range(len(connect))], axis=1),
                )
                for a in range(count)
            ]
        )
        at += len(connect)
    return lists


def pair_forces(mine, partner):
    offset = [b - a for a, b in zip(mine[:3], partner[:3])]
    distance = offset[0] * offset[0] + offset[1] * offset[1] + offset[2] * offset[2]
    weight = jnp.exp(-distance / contact_reach)
    return [
        -penalty * weight * o + damping * weight * (b - a)
        for o, a, b in zip(offset, mine[3:], partner[3:])
    ]


def choose(rows, device):
    chosen = jnp.broadcast_to(rows[0], device.shape)
    for d, row in enumerate(rows[1:], 1):
        chosen = jnp.where(device == d, row, chosen)
    return chosen


def pack_kernel(
    place_ref, speed_ref, rest_ref, mass_ref, connect_ref, modulus_ref, stiff_ref, lists_ref, patch_ref, owner_ref,
    map_ref, out_ref, mesh_ref, keep_ref, parts_ref,
):
    patches = patch_ref.shape[0]
    corners, elements = connect_ref.shape
    runs = [slice(k * LANES, (k + 1) * LANES) for k in range(elements // LANES)]
    connect = [connect_ref[:, run].astype(jnp.float32) for run in runs]
    modulus = [modulus_ref[:, run] for run in runs]
    (entries,) = elastic_entries([(place_ref[...], rest_ref[...], connect, modulus)], stiff_ref[...], parts_ref)
    keep_ref[...] = stiff_ref[...]
    out_ref[0:3, :] = place_ref[...]
    out_ref[ROW_MASS : ROW_MASS + 1, :] = mass_ref[...]
    out_ref[ROW_SPEED : ROW_SPEED + 3, :] = speed_ref[...]
    out_ref[ROW_OWNER : ROW_OWNER + 1, :] = jnp.zeros((1, LANES), jnp.float32)
    out_ref[ROW_OWNER : ROW_OWNER + 1, 0:patches] = owner_ref[...].astype(jnp.float32)
    out_ref[ROW_PATCH : ROW_PATCH + patches, :] = patch_ref[...].astype(jnp.float32)
    out_ref[ROW_PATCH + patches : ROW_PATCH + 2 * patches, :] = map_ref[...].astype(jnp.float32)
    for k in range(len(runs)):
        mesh_ref[k * corners : (k + 1) * corners, :] = connect[k]
    last = len(runs) * corners
    mesh_ref[last : last + TILE, :] = jnp.zeros((TILE, LANES), jnp.float32)
    mesh_ref[last : last + 3, :] = rest_ref[...]
    for k, scale in enumerate(modulus):
        mesh_ref[last + 4 + k : last + 5 + k, :] = scale
    out_ref[ROW_ELASTIC : ROW_ELASTIC + TILE, :] = scatter(entries)
    out_ref[ROW_LISTS : ROW_LISTS + 4, :] = lists_ref[...].astype(jnp.float32)


def route(table, rows):
    return jnp.dot(table, rows.astype(jnp.bfloat16), preferred_element_type=jnp.float32)


def put_contact(width, patches, state, indices, back, parts_ref, back_ref):
    count = width * patches
    nodes, target, device = [part.astype(jnp.int32) for part in indices]
    mine, partner = [], []
    for c in (0, 1, 2, 4, 5, 6):
        rows = [tile[c : c + 1] for tile in state]
        own = jnp.concatenate([jnp.broadcast_to(row, (patches, LANES)) for row in rows], axis=0)
        mine.append(pick(own, nodes))
        partner.append(pick(choose(rows, device), target))
    forces = pair_forces(mine, partner)
    put_parts(parts_ref, forces)
    for c, force in enumerate(forces):
        high = force.astype(jnp.bfloat16).astype(jnp.float32)
        for g, part in ((c, high), (4 + c, force - high)):
            routed = -route(back, part)
            for b in range(count // TILE):
                at = b * TILE * TILE + g * TILE
                back_ref[at : at + TILE, :] = routed[b * TILE : (b + 1) * TILE]


def contact_entries(patches, u, base, coarse_ref, fine_ref, parts_ref):
    entries = []
    for s in range(patches):
        at = u * patches + s
        entries.append((coarse_ref[pl.ds(base + at, 1), :], fine_ref[pl.ds(base + at, 1), :], get_parts(parts_ref, at)))
    return joined(entries)


def each_unit(width, unit):
    if width <= 4:
        for u in range(width):
            unit(u)
    else:
        lax.fori_loop(0, width, lambda u, carry: (unit(u), carry)[1], 0)


def face_values(tile, row):
    return pick(tile, jnp.broadcast_to(row.astype(jnp.int32), tile.shape))


def row_kernel(width, patches, where, *refs):
    total_ref, pair_ref, other_ref, keep_ref, idx_ref, link_ref, coarse_ref, fine_ref, parts_ref, back_ref = refs[-10:]
    me = lax.axis_index("my")
    side = lax.rem(lax.axis_index("mx"), 2)
    count = width * patches
    record = [refs[piece].at[place] for piece, place in where]
    state = [ref[0:TILE, :] for ref in record]
    nodes = jnp.concatenate([ref[ROW_PATCH : ROW_PATCH + patches, :] for ref in record], axis=0)
    pairs = jnp.concatenate([ref[ROW_PATCH + patches : ROW_PATCH + 2 * patches, :] for ref in record], axis=0)
    for s, ref in enumerate(record):
        keep_ref[s] = ref[0:ROW_PATCH, :]
    lane = lax.broadcasted_iota(jnp.int32, (patches, LANES), 1)
    line = lax.broadcasted_iota(jnp.int32, (patches, LANES), 0)
    owner_col = jnp.concatenate(
        [
            jnp.sum(jnp.where(lane == line, state[u][ROW_OWNER : ROW_OWNER + 1], 0.0), axis=1, keepdims=True)
            for u in range(width)
        ],
        axis=0,
    )
    row, col = [lax.broadcasted_iota(jnp.int32, (count, count), axis) for axis in (0, 1)]
    owner_row = jnp.sum(jnp.where(row == col, owner_col, 0.0), axis=0, keepdims=True)
    p, q = [(((at // patches) ^ me) * patches + at % patches).astype(jnp.float32) for at in (row, col)]
    same = owner_col == owner_row
    after = jnp.min(jnp.where(same, jnp.where(q > p, q, q + count), 3.0 * count), axis=1, keepdims=True)
    after = jnp.where(after >= count, after - count, after)
    before = jnp.max(jnp.where(same, jnp.where(q < p, q + count, q), -1.0), axis=1, keepdims=True)
    before = jnp.where(before >= count, before - count, before)
    link = jnp.where(q == after, 1.0, 0.0).astype(jnp.bfloat16)
    back = jnp.where(q == before, 1.0, 0.0)
    link_ref[...] = back
    back = back.astype(jnp.bfloat16)
    target = pick(route(link, nodes), pairs.astype(jnp.int32))
    device = jnp.broadcast_to(jnp.floor(after / patches).astype(jnp.int32) ^ me, (count, LANES)).astype(jnp.float32)
    idx_ref[0:count, :] = nodes
    idx_ref[count : 2 * count, :] = target
    idx_ref[2 * count : 3 * count, :] = device
    coarse, fine = parted(jnp.concatenate([nodes, route(back, target)], axis=0))
    coarse_ref[...] = coarse
    fine_ref[...] = fine
    put_contact(width, patches, state, (nodes, target, device), back, parts_ref, back_ref)

    def direct(u):
        info = keep_ref[u, ROW_ELASTIC : ROW_ELASTIC + TILE, :]
        total_ref[u] = scatter(contact_entries(patches, u, 0, coarse_ref, fine_ref, parts_ref), 1) + info

    def unit(u):
        info = keep_ref[u, ROW_ELASTIC : ROW_ELASTIC + TILE, :]
        total = total_ref[u] + scatter(contact_entries(patches, u, count, coarse_ref, fine_ref, back_ref), 1)
        total_ref[u] = total
        low, high = face_values(total, info[4:5]), face_values(total, info[5:6])
        pair_ref[u] = jnp.where(side == 0, high, low)[0:4]
        other_ref[u] = jnp.where(side == 0, low, high)[0:4]

    each_unit(width, direct)
    each_unit(width, unit)


def faces(tiles, lists):
    return scatter(joined([(*parted(row), tile_parts(tile)) for row, tile in zip(lists, tiles)]))


def inside(axis):
    at, size = lax.axis_index(axis), lax.axis_size(axis)
    partner = at - 1 + 2 * lax.rem(at, 2)
    return jnp.logical_and(partner >= 0, partner < size)


def mid_kernel(width, patches, keep_ref, total_ref, idx_ref, link_ref, base_ref, table_ref, list_ref, split_ref):
    me = lax.axis_index("my")
    count = width * patches
    back = link_ref[0:patches, :].astype(jnp.bfloat16)
    nodes, target, device = [idx_ref[g * count : (g + 1) * count, :] for g in range(3)]
    slot = (lax.broadcasted_iota(jnp.int32, (count, LANES), 0) // patches).astype(jnp.float32)
    table = [
        nodes[0:patches],
        route(back, target),
        target[0:patches],
        route(back, nodes),
        device[0:patches],
        route(back, slot),
    ]
    for g, rows in enumerate(table):
        table_ref[g * patches : (g + 1) * patches, :] = rows
    for g, part in enumerate(parted(jnp.concatenate(table[0:2], axis=0))):
        split_ref[g * 2 * patches : (g + 1) * 2 * patches, :] = part
    side = lax.rem(lax.axis_index("mx"), 2)

    def unit(s):
        info = keep_ref[s, 0 : 2 * TILE, :]
        u = me ^ s
        down, up = jnp.maximum(u - 1, 0) ^ me, jnp.minimum(u + 1, width - 1) ^ me
        low = face_values(total_ref[down], keep_ref[down, ROW_LISTS + 3 : ROW_LISTS + 4, :])
        high = face_values(total_ref[up], keep_ref[up, ROW_LISTS + 2 : ROW_LISTS + 3, :])
        tiles = [jnp.where(u > 0, low, 0.0), jnp.where(u < width - 1, high, 0.0)]
        total = total_ref[s] + faces(tiles, [info[ROW_LISTS + 2 : ROW_LISTS + 3], info[ROW_LISTS + 3 : ROW_LISTS + 4]])
        lists = info[ROW_LISTS : ROW_LISTS + 2]
        near, far = jnp.where(side == 0, lists[1:2], lists[0:1]), jnp.where(side == 0, lists[0:1], lists[1:2])
        list_ref[s] = jnp.concatenate([*parted(near), *parted(far)], axis=0)
        mass = info[ROW_MASS : ROW_MASS + 1]
        base_ref[s, 0:4, :] = info[0:4]
        base_ref[s, 4:7, :] = info[ROW_SPEED : ROW_SPEED + 3] + time_step * mass * total[0:3]

    each_unit(width, unit)


def mx_faces(spots, pair, other):
    tiles = [pair, jnp.where(inside("mx"), other, 0.0)]
    return scatter(joined([(spots[2 * k : 2 * k + 1], spots[2 * k + 1 : 2 * k + 2], tile_parts(tiles[k])) for k in (0, 1)]))


def elements_of(mesh, state, corners):
    last = mesh.shape[0] - TILE
    runs = last // corners
    connect = [mesh[k * corners : (k + 1) * corners] for k in range(runs)]
    return state[0:3], mesh[last : last + 3], connect, [mesh[last + 4 + k : last + 5 + k] for k in range(runs)]


def step_kernel(
    width, patches, corners, keep_ref, base_ref, pair_ref, other_ref, table_ref, list_ref, split_ref, stiff_ref, mesh_ref,
    next_ref, near_ref, send_ref, far_ref, parts_ref, element_ref,
):
    side = lax.rem(lax.axis_index("mx"), 2)
    blank = jnp.zeros((4, LANES), jnp.float32)

    def unit(s):
        base = base_ref[s]
        pair, other = [jnp.concatenate([ref[s], blank], axis=0) for ref in (pair_ref, other_ref)]
        speed = base[4:7] + time_step * base[3:4] * mx_faces(list_ref[s], pair, other)[0:3]
        next_ref[s, 0:3, :] = base[0:3] + time_step * speed
        next_ref[s, 4:7, :] = speed

    each_unit(width, unit)
    (elastic,) = elastic_entries([elements_of(mesh_ref[...], next_ref[0], corners)], stiff_ref[...], element_ref)
    table = [table_ref[g * patches : (g + 1) * patches, :] for g in range(6)]
    nodes, landing, target, from_nodes, to_slot, from_slot = [rows.astype(jnp.int32) for rows in table]
    first, second = [], []
    for c in (0, 1, 2, 4, 5, 6):
        rows = [next_ref[s, c : c + 1, :] for s in range(width)]
        home = jnp.broadcast_to(rows[0], (patches, LANES))
        first.append(jnp.concatenate([pick(home, nodes), pick(choose(rows, from_slot), from_nodes)], axis=0))
        second.append(jnp.concatenate([pick(choose(rows, to_slot), target), pick(home, landing)], axis=0))
    sign = jnp.where(lax.broadcasted_iota(jnp.int32, (2 * patches, LANES), 0) < patches, 1.0, -1.0)
    put_parts(parts_ref, [sign * force for force in pair_forces(first, second)])
    contact = [
        (split_ref[k : k + 1, :], split_ref[2 * patches + k : 2 * patches + k + 1, :], get_parts(parts_ref, k))
        for k in range(2 * patches)
    ]
    total = scatter(elastic + joined(contact))
    near_ref[...] = total
    lists = keep_ref[0, ROW_LISTS : ROW_LISTS + 4, :]
    low, high = face_values(total, lists[0:1]), face_values(total, lists[1:2])
    send_ref[...] = jnp.where(side == 0, high, low)
    far_ref[...] = jnp.where(side == 0, low, high)


def spare_kernel(
    width, patches, corners, keep_ref, next_ref, near_ref, idx_ref, link_ref, coarse_ref, fine_ref, stiff_ref,
    pair_ref, other_ref, total_ref, parts_ref, back_ref, element_ref,
):
    me = lax.axis_index("my")
    count = width * patches
    state = [next_ref[s] for s in range(width)]
    indices = [idx_ref[g * count : (g + 1) * count, :] for g in range(3)]
    put_contact(width, patches, state, indices, link_ref[...].astype(jnp.bfloat16), parts_ref, back_ref)
    around = [jnp.maximum(me - 1, 0) ^ me, jnp.minimum(me + 1, width - 1) ^ me]
    even = lax.rem(me, 2) == 0
    pair, other = pair_ref[...], other_ref[...]
    meshes = [jnp.where(even, other, pair), jnp.where(even, pair, other)]
    there = [me > 0, me < width - 1]
    units = [
        elements_of(jnp.where(exists, mesh, 0.0), next_ref[s], corners) for exists, mesh, s in zip(there, meshes, around)
    ]
    elastic = elastic_entries(units, stiff_ref[...], element_ref)
    below, above = [
        scatter(
            entries
            + contact_entries(patches, s, 0, coarse_ref, fine_ref, parts_ref)
            + contact_entries(patches, s, count, coarse_ref, fine_ref, back_ref),
            1,
        )
        for s, entries in zip(around, elastic)
    ]
    low = face_values(below, keep_ref[around[0], ROW_LISTS + 3 : ROW_LISTS + 4, :])
    high = face_values(above, keep_ref[around[1], ROW_LISTS + 2 : ROW_LISTS + 3, :])
    lists = keep_ref[0, ROW_LISTS : ROW_LISTS + 4, :]
    tiles = [jnp.where(exists, face, 0.0) for exists, face in zip(there, (low, high))]
    total_ref[...] = near_ref[...] + faces(tiles, [lists[2:3], lists[3:4]])


def end_kernel(keep_ref, list_ref, next_ref, total_ref, pair_ref, other_ref, place_ref, speed_ref):
    total = total_ref[...] + mx_faces(list_ref[0], pair_ref[...], other_ref[...])
    speed = next_ref[0, 4:7, :] + time_step * keep_ref[0, ROW_MASS : ROW_MASS + 1, :] * total[0:3]
    speed_ref[...] = speed
    place_ref[...] = next_ref[0, 0:3, :] + time_step * speed


def call(kernel, outs, scratch, *args, result=pltpu.VMEM, placed=True):
    return pl.pallas_call(
        kernel,
        out_shape=[result(shape, jnp.float32) for shape in outs],
        in_specs=[pl.BlockSpec(memory_space=pltpu.VMEM)] * len(args),
        out_specs=[pl.BlockSpec(memory_space=pltpu.VMEM)] * len(outs),
        scratch_shapes=[pltpu.VMEM(shape, jnp.float32) for shape in scratch],
        compiler_params=pltpu.CompilerParams(vmem_limit_bytes=VMEM_GRANT if placed else None),
    )(*[pltpu.with_memory_space_constraint(arg, pltpu.VMEM) if placed else arg for arg in args])


def swap(value, axis, first, other):
    size, depth = lax.axis_size(axis), lax.axis_size(other)
    axes = ("mx", "my")
    place = (lambda i, k: i * depth + k) if axis == axes[0] else (lambda i, k: k * size + i)
    pairs = []
    for i in range(size):
        partner = i + 1 - 2 * ((i - first) % 2)
        for k in range(depth):
            if 0 <= partner < size:
                pairs.append((place(i, k), place(partner, k)))
            elif depth % 2 == 0:
                pairs.append((place(i, k), place(i, k ^ 1)))
    return lax.ppermute(value, axes, pairs)


def both(pair, other):
    other = swap(other, "mx", 1, "my")
    pair = swap(pair, "mx", 0, "my")
    return pair, other


def gather_row(record, axis):
    size = lax.axis_size(axis)
    steps = [size >> k for k in range(1, size.bit_length())]

    def exchange(value, step):
        return lax.ppermute(value, axis, [(i, i ^ step) for i in range(size)])

    direct = []
    for step in steps:
        direct.append(exchange(record[None], step))
    pieces, slots = [record[None]], [[0]]
    for step, near in zip(steps, direct):
        far, far_slots = pieces[1:], [s ^ step for held in slots[1:] for s in held]
        pieces, slots = pieces + [near], slots + [[step]]
        if far:
            pieces.append(exchange(far[0] if len(far) == 1 else jnp.concatenate(far, axis=0), step))
            slots.append(far_slots)
    where = {s: (n, k) for n, held in enumerate(slots) for k, s in enumerate(held)}
    return pieces, [where[s] for s in range(size)]


def body(
    positions, velocities, rest_positions, inverse_mass, element_nodes, modulus, stiffness, shared_lists, patch_nodes,
    patch_owner, pair_map,
):
    width = lax.axis_size("my")
    patches = patch_owner.shape[0]
    corners, elements = element_nodes.shape
    count = width * patches
    modulus, mass = modulus[None], inverse_mass[None]
    runs = elements // LANES
    element_parts = (TILE * corners * runs, LANES)
    tile = (TILE, LANES)
    parts = (TILE * count, LANES)
    record, mesh, stiff = call(
        pack_kernel,
        [(ROW_PATCH + 2 * patches, LANES), (runs * corners + TILE, LANES), stiffness.shape],
        [element_parts],
        positions, velocities, rest_positions, mass, element_nodes, modulus, stiffness, shared_lists, patch_nodes,
        patch_owner[None], pair_map, placed=False,
    )
    pieces, where = gather_row(record, "my")
    kept = (width, ROW_PATCH, LANES)
    mesh_pair = swap(mesh, "my", 0, "mx")
    mesh_other = swap(mesh, "my", 1, "mx")
    total, pair, other, keep, indices, link, *spots = call(
        functools.partial(row_kernel, width, patches, where),
        [(width, TILE, LANES), (width, 4, LANES), (width, 4, LANES), kept, (3 * count, LANES), (count, count)]
        + [(2 * count, LANES)] * 2,
        [parts, parts],
        *pieces,
    )
    states = (width, TILE, LANES)
    pair, other = both(pair, other)
    base, table, lists, split = call(
        functools.partial(mid_kernel, width, patches),
        [states, (6 * patches, LANES), (width, 4, LANES), (4 * patches, LANES)],
        [],
        keep, total, indices, link,
    )
    contact = functools.partial(step_kernel, width, patches, corners)
    state, near, pair, other = call(
        contact,
        [states, tile, tile, tile],
        [(TILE * 2 * patches, LANES), element_parts],
        keep, base, pair, other, table, lists, split, stiff, mesh,
    )
    pair, other = both(pair, other)
    (total,) = call(
        functools.partial(spare_kernel, width, patches, corners),
        [tile],
        [parts, parts, (2 * element_parts[0], LANES)],
        keep, state, near, indices, link, *spots, stiff, mesh_pair, mesh_other,
    )
    outs = [(3, LANES), (3, LANES)]
    return tuple(call(end_kernel, outs, [], keep, lists, state, total, pair, other, result=jax.ShapeDtypeStruct))


def solution(mesh):
    in_specs = (
        P(None, ("mx", "my")),
        P(None, ("mx", "my")),
        P(None, ("mx", "my")),
        P(("mx", "my")),
        P(None, ("mx", "my")),
        P(("mx", "my")),
        P(),
        P(None, ("mx", "my")),
        P(("mx", "my"), None),
        P(("mx", "my")),
        P(("mx", "my"), None),
    )
    out_specs = (P(None, ("mx", "my")), P(None, ("mx", "my")))
    return jax.shard_map(body, mesh=mesh, in_specs=in_specs, out_specs=out_specs, check_vma=False)
```
